32 devices in a mesh: groups: 2 (over x), rows: 16 (over z, y, core).
Axes of the slice: x: 2, y: 2, z: 4, core: 2. Of those that a mesh axis runs over, the one named last changes fastest.
Arguments:
- points: bfloat16 [64, 32768], P(None, ('groups', 'rows')), parts along dimension 1, may hold values from -12 to 12
- landmarks: bfloat16 [64, 2048], P(None, 'groups'), parts along dimension 1, may hold values from -12 to 12
- chol: float32 [2048, 1024], P('groups'), parts along dimension 0, as said below
- ridge: float32 [2], P('groups'), parts along dimension 0, may hold values from 0.5 to 2
- solution: float32 [8, 32768], P(None, ('groups', 'rows')), parts along dimension 1, may hold values from -6 to 6
- residual: float32 [8, 32768], P(None, ('groups', 'rows')), parts along dimension 1, may hold values from -6 to 6
- direction: float32 [8, 32768], P(None, ('groups', 'rows')), parts along dimension 1, may hold values from -6 to 6
- rz_prev: float32 [16], P('groups'), parts along dimension 0, may hold values from 8192 to 32768
Outputs:
- solution_new: float32 [8, 32768], P(None, ('groups', 'rows')), parts along dimension 1
- residual_new: float32 [8, 32768], P(None, ('groups', 'rows')), parts along dimension 1
- direction_new: float32 [8, 32768], P(None, ('groups', 'rows')), parts along dimension 1
- inner_new: float32 [16], P('groups'), parts along dimension 0
The draws below stay inside these ranges and needn't reach their ends.
There are 2 independent parts, one for each index of `groups`. The reference program is written for one: setup_inputs(seed, part) draws one part's arguments, and reference() takes and returns one part's arrays. A program takes and returns all parts, laid end to end along the dimension named above; each array names one. Nothing has to cross between parts.
Inputs may be any that keep to these rules, and one draw needn't show every extreme that they name: chol is lower triangular with a positive diagonal, and chol chol^T = ridge k(landmarks, landmarks) + cross^T cross, with k and cross as in the reference program.
All inputs are finite; a program needn't handle non-finite values.
Results may differ from the reference program's by a relative error of at most 0.0064.
Values may be sent and summed in bfloat16 or wider, within the bound.
A program may use at most 64 MiB of HBM per device.

```python
import math
import jax
import jax.numpy as jnp
from jax import lax

FEAT = 64
OUTS = 8
LAND = 1024
NPTS = 16384


latent_dims = 8


def shared_sample(key):
    base = jax.random.fold_in(key, 23)
    keys = jax.random.split(base, 6)
    basis = jnp.clip(jax.random.normal(keys[0], (FEAT, latent_dims), jnp.float32), -3.0, 3.0)
    spread = 0.5
    latent_points = jax.random.uniform(keys[1], (latent_dims, NPTS), jnp.float32, -1.5, 1.5)
    latent_marks = jax.random.uniform(keys[2], (latent_dims, LAND), jnp.float32, -1.5, 1.5)
    ridge_value = jnp.exp(jax.random.uniform(keys[5], (1,), jnp.float32, math.log(0.5), math.log(2.0)))
    noise_points = spread * jnp.clip(jax.random.normal(keys[3], (FEAT, NPTS), jnp.float32), -4.0, 4.0)
    noise_marks = spread * jnp.clip(jax.random.normal(keys[4], (FEAT, LAND), jnp.float32), -4.0, 4.0)
    points = jnp.clip(jnp.dot(basis, latent_points, precision=lax.Precision.HIGHEST) + noise_points, -12.0, 12.0)
    landmarks = jnp.clip(jnp.dot(basis, latent_marks, precision=lax.Precision.HIGHEST) + noise_marks, -12.0, 12.0)
    return (points, landmarks, ridge_value)


def square_sums(values):
    return jnp.sum(values * values, axis=0)


def gauss_kernel(left, right):
    inner = jnp.dot(left.T, right, precision=lax.Precision.HIGHEST)
    dist = square_sums(left)[:, None] + square_sums(right)[None, :] - 2.0 * inner
    return jnp.exp(-dist / (2.0 * FEAT))


def draw_points(key, part):
    return shared_sample(key)[0].astype(jnp.bfloat16)


def draw_landmarks(key, part):
    return shared_sample(key)[1].astype(jnp.bfloat16)


def draw_ridge(key, part):
    return shared_sample(key)[2].astype(jnp.float32)


def draw_chol(key, part):
    points, landmarks, ridge_value = shared_sample(key)
    rounded_points = points.astype(jnp.bfloat16).astype(jnp.float32)
    rounded_marks = landmarks.astype(jnp.bfloat16).astype(jnp.float32)
    cross = gauss_kernel(rounded_points, rounded_marks)
    inner = ridge_value[0] * gauss_kernel(rounded_marks, rounded_marks)
    inner = inner + jnp.dot(cross.T, cross, precision=lax.Precision.HIGHEST)
    inner = 0.5 * (inner + inner.T)
    return jnp.linalg.cholesky(inner).astype(jnp.float32)


def block_levels(rng, extent, cuts, smallest, top_value):
    loudness = 1.0
    for position, shards_of in cuts:
        draws = jax.random.uniform(jax.random.fold_in(jax.random.fold_in(rng, 6), position), (shards_of,), jnp.float32, smallest / len(cuts), top_value / len(cuts))
        loudness = loudness * jnp.repeat(jnp.exp(draws), extent[position] // shards_of).reshape((-1,) + (1,) * (len(extent) - 1 - position))
    return loudness


def gaussian(rng, dims, width, bound, shards=(), held_as=jnp.bfloat16):
    gain = block_levels(rng, dims, shards, -0.22, 0.18) if shards else 1.0
    values = jax.random.normal(rng, dims, jnp.float32) * width * gain
    return jnp.minimum(jnp.maximum(values, -bound), bound).astype(held_as)


def setup_inputs(seed: int = 0, part: int = 0) -> dict:
    splits = jax.random.split(jax.random.key(seed), 9)
    part_keys = jax.random.split(jax.random.fold_in(splits[8], part), 9)
    return {
        "points": draw_points(jax.random.fold_in(jax.random.fold_in(splits[8], part), 71), part),
        "landmarks": draw_landmarks(jax.random.fold_in(jax.random.fold_in(splits[8], part), 71), part),
        "chol": draw_chol(jax.random.fold_in(jax.random.fold_in(splits[8], part), 71), part),
        "ridge": draw_ridge(jax.random.fold_in(jax.random.fold_in(splits[8], part), 71), part),
        "solution": gaussian(part_keys[4], (OUTS, NPTS), 1.0, 6.0, ((1, 16),), jnp.float32),
        "residual": gaussian(part_keys[5], (OUTS, NPTS), 1.0, 6.0, ((1, 16),), jnp.float32),
        "direction": gaussian(part_keys[6], (OUTS, NPTS), 1.0, 6.0, ((1, 16),), jnp.float32),
        "rz_prev": jnp.clip(jnp.exp(jax.random.uniform(part_keys[7], (OUTS,), jnp.float32, math.log(8192.0), math.log(32768.0))), 8192.0, 32768.0),
    }


def square_norms(features):
    wide = features.astype(jnp.float32)
    return jnp.sum(wide * wide, axis=0)

def kernel_block(row_points, row_norms, col_points, col_norms):
    scale = 0.5 / row_points.shape[0]
    cross = lax.dot_general(row_points.astype(jnp.float32), col_points.astype(jnp.float32), (((0,), (0,)), ((), ())), preferred_element_type=jnp.float32)
    dist = row_norms[:, None] + col_norms[None, :] - 2.0 * cross
    return jnp.exp(-scale * dist)

def reference(points, landmarks, chol, ridge, solution, residual, direction, rz_prev):
    ridge_value = ridge[0]
    norms = square_norms(points)
    landmark_norms = square_norms(landmarks)
    landmark_kernel = kernel_block(points, norms, landmarks, landmark_norms)
    projection = jnp.dot(residual, landmark_kernel, precision=lax.Precision.HIGHEST)
    coeffs = jax.scipy.linalg.cho_solve((chol, True), projection.T)
    precond = (residual - jnp.dot(coeffs.T, landmark_kernel.T, precision=lax.Precision.HIGHEST)) / ridge_value
    inner_new = jnp.sum(precond * residual, axis=1)
    direction_new = precond + (inner_new / rz_prev)[:, None] * direction
    direction_low = direction_new.astype(jnp.bfloat16)
    total = points.shape[1]
    block_len = math.gcd(total, 512)
    blocks = total // block_len
    feature_count = points.shape[0]
    point_blocks = jnp.moveaxis(points.reshape(feature_count, blocks, block_len), 1, 0)
    norm_blocks = norms.reshape(blocks, block_len)

    def one_block(inputs):
        block_points, block_norms = inputs
        kernel_tile = kernel_block(block_points, block_norms, points, norms).astype(jnp.bfloat16)
        return lax.dot_general(direction_low.astype(jnp.float32), kernel_tile.astype(jnp.float32), (((1,), (1,)), ((), ())), preferred_element_type=jnp.float32)
    stacked = lax.map(one_block, (point_blocks, norm_blocks))
    kernel_part = jnp.moveaxis(stacked, 0, 1).reshape(direction_new.shape[0], total)
    image = kernel_part + ridge_value * direction_new
    curvature = jnp.sum(direction_new * image, axis=1)
    alpha = inner_new / curvature
    solution_new = solution + alpha[:, None] * direction_new
    residual_new = residual - alpha[:, None] * image
    return (solution_new, residual_new, direction_new, inner_new)
```

```python
import functools
import math

import jax
import jax.numpy as jnp
from jax import lax
from jax.experimental import pallas as pl
from jax.experimental.pallas import tpu as pltpu
from jax.sharding import PartitionSpec as P

HIGH = lax.Precision.HIGHEST
TILE = 128
CHUNK = 256
GROUP = 2 * TILE
STORED_BLOCKS = 16


def dot_nn(left, right, precision=None):
    return lax.dot_general(
        left, right, (((1,), (0,)), ((), ())), precision=precision, preferred_element_type=jnp.float32
    )


def dot_nt(left, right, precision=None):
    return lax.dot_general(
        left, right, (((1,), (1,)), ((), ())), precision=precision, preferred_element_type=jnp.float32
    )


def dot_tn(left, right):
    return lax.dot_general(
        left, right, (((0,), (0,)), ((), ())), preferred_element_type=jnp.float32
    )


def split(values):
    top = values.astype(jnp.bfloat16).astype(jnp.float32)
    rest = values - top
    mid = rest.astype(jnp.bfloat16).astype(jnp.float32)
    return top, mid, rest - mid


def store_split(ref, at, values):
    for term, part in enumerate(split(values)):
        ref[(term,) + at] = part.astype(jnp.bfloat16)


def dot_split(left, parts, dot):
    outs = left.shape[0]
    stacked = jnp.concatenate(split(left), axis=0).astype(jnp.bfloat16)
    high = dot(stacked, parts[0])
    mid = dot(stacked[:2 * outs], parts[1])
    low = dot(stacked[:2 * outs], parts[2])
    small = low[:outs] + mid[outs:] + high[2 * outs:]
    return high[:outs] + (high[outs:2 * outs] + mid[:outs] + small)


def norm_rows(features, first):
    wide = features.astype(jnp.float32)
    half = -0.5 * jnp.sum(wide * wide, axis=0, keepdims=True)
    top = half.astype(jnp.bfloat16).astype(jnp.float32)
    rest = half - top
    mid = rest.astype(jnp.bfloat16).astype(jnp.float32)
    low = rest - mid
    row = lax.broadcasted_iota(jnp.int32, (16, features.shape[1]), 0)
    at = 0 if first else 3
    ones = 3 - at
    rows = jnp.where((row >= ones) & (row < ones + 3), 1.0, 0.0)
    rows = jnp.where(row == at, top, rows)
    rows = jnp.where(row == at + 1, mid, rows)
    rows = jnp.where(row == at + 2, low, rows)
    return rows.astype(jnp.bfloat16)


def eye_mask(width):
    shape = (8, width)
    return lax.broadcasted_iota(jnp.int32, shape, 0) == lax.broadcasted_iota(jnp.int32, shape, 1)


def to_row(column, width):
    return jnp.sum(jnp.where(eye_mask(width), column, 0.0), axis=0, keepdims=True)


def to_column(row):
    return jnp.sum(jnp.where(eye_mask(row.shape[1]), row, 0.0), axis=1, keepdims=True)


def kernel(
    n,
    keep,
    points_ref,
    landmarks_ref,
    chol_hbm,
    ridge_ref,
    residual_ref,
    direction_ref,
    rz_ref,
    image_out,
    direction_out,
    inner_out,
    alpha_out,
    chol,
    chol_parts,
    inverse_parts,
    inverse,
    points,
    own_aug,
    side_aug,
    col_aug,
    cross,
    kernel_store,
    rs_send,
    rs_recv,
    ag,
    proj,
    work,
    dirs,
    acc,
    side_recv,
    img_send,
    img_recv,
    curv_buf,
    chol_sem,
    rs_sems,
    ag_sems,
    dir_sems,
    curv_sems,
    img_sems,
    side_sems,
    point_recv,
    point_fwd,
    own_sems,
    share_sems,
):
    me = lax.axis_index("rows")
    feat, local = points_ref.shape
    land = landmarks_ref.shape[1]
    outs = residual_ref.shape[0]
    chips = n // 2
    half = chips // 2
    core = me % 2
    chip = me // 2
    odd = chip % 2
    pos = (1 - odd) * (chip // 2) + odd * (chips - (chip + 1) // 2)
    scale = math.log2(math.e) / feat

    def row_of(position, lane):
        position = (position + chips) % chips
        upper = position // half
        at = (1 - upper) * (2 * position) + upper * (2 * chips - 1 - 2 * position)
        return at * 2 + (core + lane) % 2

    def remote(src, dst, send, recv, to):
        return pltpu.make_async_remote_copy(
            src_ref=src,
            dst_ref=dst,
            send_sem=send,
            recv_sem=recv,
            device_id={"rows": to},
            device_id_type=pl.DeviceIdType.MESH,
        )

    def others(body):
        lax.fori_loop(1, n, lambda k, carry: (body((me + k) % n), carry)[1], 0)

    def send_all(src_of, buf, sems):
        others(lambda to: remote(src_of(to), buf.at[me], sems.at[0, to], sems.at[1, me], to).start())

    def wait_all(src_of, buf, sems):
        others(lambda to: remote(src_of(to), buf.at[to], sems.at[0, to], sems.at[1, to], to).wait_recv())

    def drain(src_of, buf, sems):
        others(lambda to: remote(src_of(to), buf.at[me], sems.at[0, to], sems.at[1, me], to).wait_send())

    chol_copy = pltpu.make_async_copy(chol_hbm, chol, chol_sem)
    chol_copy.start()

    barrier = pltpu.get_barrier_semaphore()
    others(lambda to: pl.semaphore_signal(
        barrier, inc=1, device_id={"rows": to}, device_id_type=pl.DeviceIdType.MESH))

    upper = pos // half
    partner = row_of(pos, 1)
    left = row_of(pos - 1, 0)
    left_last = row_of(pos - 1, ((pos - 1 + chips) % chips) // half)
    across = row_of(pos + half, upper)
    taker = row_of(pos + half, 1 - upper)

    def near(k):
        return row_of(pos + k, 0)

    def back(k):
        return row_of(pos - k, 0)

    def hop(k, src, owner, to):
        return remote(src, points.at[owner], point_fwd.at[k], point_recv.at[owner], to)

    own_left = hop(0, points_ref, me, left if half > 1 else left_last)
    own_side = remote(points_ref, points.at[me], own_sems.at[0], point_recv.at[me], partner)

    own_aug[0:feat, :] = points_ref[...]
    own_aug[feat:, :] = norm_rows(points_ref[...], True)
    col_aug[0:feat, :] = landmarks_ref[...]
    col_aug[feat:, :] = norm_rows(landmarks_ref[...], False)

    def entries(left_aug, at, right_aug):
        return jnp.exp2(dot_tn(left_aug[:, pl.ds(at, CHUNK)], right_aug[...]) * scale)

    proj[...] = jnp.zeros_like(proj)

    def project(i, carry):
        at = pl.multiple_of(i * CHUNK, CHUNK)
        store_split(cross, (pl.ds(at, CHUNK), slice(None)), entries(own_aug, at, col_aug))
        parts = [cross[term, pl.ds(at, CHUNK), :] for term in range(3)]
        proj[...] += dot_split(residual_ref[:, pl.ds(at, CHUNK)], parts, dot_nn)
        return carry

    lax.fori_loop(0, local // CHUNK, project, 0)
    own_square = to_row(jnp.sum(residual_ref[...] * residual_ref[...], axis=1, keepdims=True), TILE)

    pl.semaphore_wait(barrier, n - 1)

    tiles = land // TILE
    groups = land // GROUP
    rows_per = outs * tiles // n
    for piece in range(n):
        h, j = piece // tiles, piece % tiles
        rs_send[piece, 0:rows_per] = proj[h * rows_per:(h + 1) * rows_per, j * TILE:(j + 1) * TILE]
        rs_send[piece, rows_per:rows_per + 1] = own_square
    send_all(lambda to: rs_send.at[to], rs_recv, rs_sems)
    rs_recv[me, 0:rows_per + 1] = rs_send[me, 0:rows_per + 1]
    own_left.start()
    own_side.start()

    def make_left(owner_points):
        col_aug[0:feat, :] = owner_points[...]
        col_aug[feat:, :] = norm_rows(owner_points[...], False)

    def make_block(slot, right_aug):
        for at in range(0, local, CHUNK):
            kernel_store[slot, at:at + CHUNK, :] = entries(col_aug, at, right_aug).astype(jnp.bfloat16)

    chol_copy.wait()

    row = lax.broadcasted_iota(jnp.int32, (TILE, TILE), 0)
    col = lax.broadcasted_iota(jnp.int32, (TILE, TILE), 1)

    share = tiles // 2
    first = core * share

    def own_block(b):
        at = pl.multiple_of((first + b) * TILE, TILE)
        return chol[pl.ds(at, TILE), pl.ds(at, TILE)]

    inverted = [jnp.where(row == col, 1.0 / own_block(b), 0.0) for b in range(share)]
    size = 1
    while size < TILE:
        below = (row // size == col // size + 1) & (row // (2 * size) == col // (2 * size))
        for b in range(share):
            off = jnp.where(below, own_block(b), 0.0)
            if size == 1:
                on_row = jnp.sum(inverted[b], axis=1, keepdims=True)
                on_col = jnp.sum(inverted[b], axis=0, keepdims=True)
                change = on_row * off * on_col
            else:
                change = dot_nn(dot_nn(inverted[b], off, HIGH), inverted[b], HIGH)
            inverted[b] = inverted[b] - change
        size *= 2
    for b in range(share):
        inverse[first + b] = inverted[b]

    wait_all(lambda to: rs_send.at[to], rs_recv, rs_sems)
    gathered = jnp.sum(rs_recv[:, 0:rows_per + 1], axis=0)
    ag[me] = gathered[0:rows_per]
    square = to_column(gathered[rows_per:rows_per + 1])
    send_all(lambda to: ag.at[me], ag, ag_sems)

    shares = inverse.at[pl.ds(first, share)]
    shared = remote(shares, shares, share_sems.at[0], share_sems.at[1], partner)
    shared.start()

    def pass_on(k):
        owner = near(k)
        to = left_last if k == half - 1 else left
        hop(k, points.at[owner], owner, left).wait_recv()
        hop(k, points.at[owner], owner, to).start()

    def pass_on_any(k):
        owner = near(k)
        hop(k, points.at[owner], owner, left).wait_recv()

        @pl.when(k < half - 1)
        def _():
            hop(k, points.at[owner], owner, left).start()

        @pl.when(k == half - 1)
        def _():
            hop(k, points.at[owner], owner, left_last).start()

    own_slot, side_slot, across_slot = 2 * half - 1, 2 * half, 2 * half - 2

    if half > 1:
        pass_on(1)
    remote(points_ref, points.at[partner], own_sems.at[0], point_recv.at[partner], partner).wait_recv()
    side_aug[0:feat, :] = points[partner]
    side_aug[feat:, :] = norm_rows(points[partner], True)
    if keep:
        make_left(points_ref)
        make_block(own_slot, own_aug)

    other = inverse.at[pl.ds(share - first, share)]
    remote(other, other, share_sems.at[0], share_sems.at[1], partner).wait_recv()
    for b in range(groups):
        upper_block, lower_block = inverse[2 * b], inverse[2 * b + 1]
        at, end = b * GROUP, (b + 1) * GROUP
        off = chol[at + TILE:end, at:at + TILE]
        change = dot_nn(dot_nn(lower_block, off, HIGH), upper_block, HIGH)
        zero = jnp.zeros_like(upper_block)
        whole = jnp.concatenate(
            [jnp.concatenate([upper_block, zero], axis=1), jnp.concatenate([-change, lower_block], axis=1)], axis=0
        )
        store_split(inverse_parts, (b,), whole)
        if b > 0:
            store_split(chol_parts, (slice(at, end), slice(0, at)), chol[at:end, :at])

    if keep:
        make_left(points.at[partner])
        make_block(side_slot, own_aug)
    if half > 2:
        pass_on(2)
    wait_all(lambda to: ag.at[me], ag, ag_sems)
    for piece in range(n):
        h, j = piece // tiles, piece % tiles
        work[h * rows_per:(h + 1) * rows_per, j * TILE:(j + 1) * TILE] = ag[piece]
    pieces = [work[:, b * GROUP:(b + 1) * GROUP] for b in range(groups)]

    def block_parts(i, j):
        rows, cols = slice(i * GROUP, (i + 1) * GROUP), slice(j * GROUP, (j + 1) * GROUP)
        return [chol_parts[term, rows, cols] for term in range(3)]

    def inverse_of(b):
        return [inverse_parts[term, b] for term in range(3)]

    for b in range(groups):
        pieces[b] = dot_split(pieces[b], inverse_of(b), dot_nt)
        for i in range(b + 1, groups):
            pieces[i] = pieces[i] - dot_split(pieces[b], block_parts(i, b), dot_nt)
    halfway = jnp.concatenate(pieces, axis=1)
    for b in reversed(range(groups)):
        pieces[b] = dot_split(pieces[b], inverse_of(b), dot_nn)
        for j in reversed(range(b)):
            pieces[j] = pieces[j] - dot_split(pieces[b], block_parts(b, j), dot_nn)
    coeffs = jnp.concatenate(pieces, axis=1)

    ridge = ridge_ref[0]
    inner = (square - jnp.sum(halfway * halfway, axis=1, keepdims=True)) / ridge
    inner_out[...] = to_row(inner, TILE)[:, :outs]
    residual = residual_ref[...]
    precond = (residual - dot_split(coeffs, [cross.at[term][...] for term in range(3)], dot_nt)) / ridge
    direction_new = precond + (inner / to_column(rz_ref[...])) * direction_ref[...]
    direction_out[...] = direction_new
    dirs[me] = direction_new.astype(jnp.bfloat16)

    def dir_to(to):
        return remote(dirs.at[me], dirs.at[to], dir_sems.at[0, to], dir_sems.at[1, me], to)

    def send_dir(to):
        remote(dirs.at[me], dirs.at[me], dir_sems.at[0, to], dir_sems.at[1, me], to).start()

    def wait_dir(src):
        remote(dirs.at[me], dirs.at[src], dir_sems.at[0, src], dir_sems.at[1, src], src).wait_recv()

    send_dir(taker)
    lax.fori_loop(1, half, lambda k, carry: (send_dir(back(half - k)), carry)[1], 0)
    send_dir(partner)

    def wait_across():
        hop(0, points.at[across], across, left).wait_recv()

    def make_pair(k, slot):
        make_left(points.at[near(k)])
        make_block(slot, own_aug)
        make_block(slot + 1, side_aug)

    acc[...] = jnp.zeros_like(acc)

    def forward(owner, slot, side):
        acc[1] += dot_nn(dirs[owner], kernel_store[slot])
        if side:
            acc[2] += dot_nn(dirs[owner], kernel_store[slot + 1])

    def image_to(k, owner):
        return remote(img_send.at[k], img_recv.at[k], img_sems.at[0, k], img_sems.at[1, k], owner)

    def backward(k, owner, slot, side):
        total = dot_nt(dirs[me], kernel_store[slot])
        if side:
            total = total + dot_nt(dirs[partner], kernel_store[slot + 1])
        img_send[k] = total
        image_to(k, owner).start()

    def at_own():
        acc[0] += dot_nn(dirs[me], kernel_store[own_slot if keep else 0])

    def at_side():
        acc[0] += dot_nn(dirs[partner], kernel_store[side_slot if keep else 0])

    if keep:
        for k in range(3, half):
            pass_on(k)

        def build(k, carry):
            make_pair(k, 2 * (k - 1))
            return carry

        lax.fori_loop(1, half, build, 0)
        wait_across()
        make_left(points.at[across])
        make_block(across_slot, own_aug)

        at_own()
        wait_dir(partner)
        at_side()

        def ahead(k, carry):
            wait_dir(near(k))
            forward(near(k), 2 * (k - 1), True)
            return carry

        lax.fori_loop(1, half, ahead, 0)
        wait_dir(across)
        forward(across, across_slot, False)
    else:
        make_left(points_ref)
        make_block(0, own_aug)
        at_own()
        make_left(points.at[partner])
        make_block(0, own_aug)
        wait_dir(partner)
        at_side()

        def both(k, carry):
            @pl.when(k > 2)
            def _():
                pass_on_any(k)

            make_pair(k, 0)
            wait_dir(near(k))
            forward(near(k), 0, True)
            backward(k - 1, near(k), 0, True)
            return carry

        lax.fori_loop(1, half, both, 0)
        wait_across()
        make_left(points.at[across])
        make_block(0, own_aug)
        wait_dir(across)
        forward(across, 0, False)
        backward(half - 1, across, 0, False)

    side_send = remote(acc.at[2], side_recv, side_sems.at[0], side_sems.at[1], partner)
    side_send.start()
    direction_new = direction_out[...]
    once = direction_new * (acc[0] + 2.0 * acc[1] + ridge * direction_new)
    twice = once + 2.0 * dirs[partner].astype(jnp.float32) * acc[2]
    curv_buf[me] = to_row(jnp.sum(twice, axis=1, keepdims=True), TILE)
    send_all(lambda to: curv_buf.at[me], curv_buf, curv_sems)

    if keep:
        backward(half - 1, across, across_slot, False)

        def behind(i, carry):
            k = half - i
            backward(k - 1, near(k), 2 * (k - 1), True)
            return carry

        lax.fori_loop(1, half, behind, 0)

    side_send.wait_recv()
    image = acc[0] + acc[1] + ridge * direction_new + side_recv[...]

    drain(lambda to: rs_send.at[to], rs_recv, rs_sems)
    drain(lambda to: ag.at[me], ag, ag_sems)
    shared.wait_send()
    own_left.wait_send()
    own_side.wait_send()

    def relay_drain(k, carry):
        hop(k, points.at[near(k)], near(k), left).wait_send()
        return carry

    lax.fori_loop(1, half, relay_drain, 0)

    def dir_drain(k, carry):
        dir_to(back(k)).wait_send()
        return carry

    lax.fori_loop(1, half, dir_drain, 0)
    dir_to(taker).wait_send()
    dir_to(partner).wait_send()

    for k in range(half):
        image_to(k, across).wait_recv()
        image = image + img_recv[k]
    image_out[...] = image

    wait_all(lambda to: curv_buf.at[me], curv_buf, curv_sems)
    alpha_out[...] = inner_out[...] / jnp.sum(curv_buf[...], axis=0)[:, :outs]
    drain(lambda to: curv_buf.at[me], curv_buf, curv_sems)
    side_send.wait_send()
    for k in range(half):
        image_to(k, across).wait_send()


def finish(
    image_ref,
    direction_ref,
    inner_ref,
    alpha_ref,
    solution_ref,
    residual_ref,
    solution_out,
    residual_out,
    direction_out,
    inner_out,
):
    alpha = to_column(alpha_ref[...])
    direction = direction_ref[...]
    solution_out[...] = solution_ref[...] + alpha * direction
    residual_out[...] = residual_ref[...] - alpha * image_ref[...]
    direction_out[...] = direction
    inner_out[...] = inner_ref[...]


def solution(mesh):
    n = mesh.shape["rows"]

    def local(points, landmarks, chol, ridge, solution, residual, direction, rz_prev):
        feat, own = points.shape
        land = landmarks.shape[1]
        outs = residual.shape[0]
        keep = n <= STORED_BLOCKS
        half = n // 4
        piece = outs * land // (TILE * n)
        padded = -(-(piece + 1) // 8) * 8
        f32, bf16 = jnp.float32, jnp.bfloat16
        vmem = pl.BlockSpec(memory_space=pltpu.VMEM)
        wide = jax.ShapeDtypeStruct((outs, own), f32)
        thin = jax.ShapeDtypeStruct((1, outs), f32)
        dma = pltpu.SemaphoreType.DMA
        results = pl.pallas_call(
            functools.partial(kernel, n, keep),
            out_shape=(wide, wide, thin, thin),
            in_specs=[
                vmem,
                vmem,
                pl.BlockSpec(memory_space=pl.ANY),
                pl.BlockSpec(memory_space=pltpu.SMEM),
                vmem,
                vmem,
                vmem,
            ],
            out_specs=(vmem,) * 4,
            scratch_shapes=[
                pltpu.VMEM((land, land), f32),
                pltpu.VMEM((3, land, land), bf16),
                pltpu.VMEM((3, land // GROUP, GROUP, GROUP), bf16),
                pltpu.VMEM((land // TILE, TILE, TILE), f32),
                pltpu.VMEM((n, feat, own), bf16),
                pltpu.VMEM((feat + 16, own), bf16),
                pltpu.VMEM((feat + 16, own), bf16),
                pltpu.VMEM((feat + 16, own), bf16),
                pltpu.VMEM((3, own, land), bf16),
                pltpu.VMEM((2 * half + 1 if keep else 2, own, own), bf16),
                pltpu.VMEM((n, padded, TILE), f32),
                pltpu.VMEM((n, padded, TILE), f32),
                pltpu.VMEM((n, piece, TILE), f32),
                pltpu.VMEM((outs, land), f32),
                pltpu.VMEM((outs, land), f32),
                pltpu.VMEM((n, outs, own), bf16),
                pltpu.VMEM((3, outs, own), f32),
                pltpu.VMEM((outs, own), f32),
                pltpu.VMEM((half, outs, own), f32),
                pltpu.VMEM((half, outs, own), f32),
                pltpu.VMEM((n, 1, TILE), f32),
                dma,
                dma((2, n)),
                dma((2, n)),
                dma((2, n)),
                dma((2, n)),
                dma((2, half)),
                dma((2,)),
                dma((n,)),
                dma((half,)),
                dma((2,)),
                dma((2,)),
            ],
            compiler_params=pltpu.CompilerParams(
                collective_id=0, has_side_effects=True, vmem_limit_bytes=62 * 1024 * 1024
            ),
            name="cg_step",
        )(points, landmarks, chol, ridge, residual, direction, rz_prev.reshape(1, outs))
        results = pl.pallas_call(
            finish,
            out_shape=(wide, wide, wide, thin),
            in_specs=[vmem] * 6,
            out_specs=(vmem,) * 4,
            name="finish",
        )(*results, solution, residual)
        return (results[0], results[1], results[2], results[3].reshape(outs))

    wide_spec = P(None, ("groups", "rows"))
    in_specs = (
        wide_spec,
        P(None, "groups"),
        P("groups", None),
        P("groups"),
        wide_spec,
        wide_spec,
        wide_spec,
        P("groups"),
    )
    out_specs = (wide_spec, wide_spec, wide_spec, P("groups"))
    return jax.shard_map(local, mesh=mesh, in_specs=in_specs, out_specs=out_specs, check_vma=False)
```

```python
import functools
import math

import jax
import jax.numpy as jnp
from jax import lax
from jax.experimental import pallas as pl
from jax.experimental.pallas import tpu as pltpu
from jax.sharding import PartitionSpec as P

HIGH = lax.Precision.HIGHEST
TILE = 128
CHUNK = 256
GROUP = 2 * TILE
STORED_BLOCKS = 16


def dot_nn(left, right, precision=None):
    return lax.dot_general(
        left, right, (((1,), (0,)), ((), ())), precision=precision, preferred_element_type=jnp.float32
    )


def dot_nt(left, right, precision=None):
    return lax.dot_general(
        left, right, (((1,), (1,)), ((), ())), precision=precision, preferred_element_type=jnp.float32
    )


def dot_tn(left, right):
    return lax.dot_general(
        left, right, (((0,), (0,)), ((), ())), preferred_element_type=jnp.float32
    )


def split(values):
    top = values.astype(jnp.bfloat16).astype(jnp.float32)
    rest = values - top
    mid = rest.astype(jnp.bfloat16).astype(jnp.float32)
    return top, mid, rest - mid


def store_split(ref, at, values):
    for term, part in enumerate(split(values)):
        ref[(term,) + at] = part.astype(jnp.bfloat16)


def dot_split(left, parts, dot):
    outs = left.shape[0]
    stacked = jnp.concatenate(split(left), axis=0).astype(jnp.bfloat16)
    high = dot(stacked, parts[0])
    mid = dot(stacked[:2 * outs], parts[1])
    low = dot(stacked[:2 * outs], parts[2])
    small = low[:outs] + mid[outs:] + high[2 * outs:]
    return high[:outs] + (high[outs:2 * outs] + mid[:outs] + small)


def norm_rows(features, first):
    wide = features.astype(jnp.float32)
    half = -0.5 * jnp.sum(wide * wide, axis=0, keepdims=True)
    top = half.astype(jnp.bfloat16).astype(jnp.float32)
    rest = half - top
    mid = rest.astype(jnp.bfloat16).astype(jnp.float32)
    low = rest - mid
    row = lax.broadcasted_iota(jnp.int32, (16, features.shape[1]), 0)
    at = 0 if first else 3
    ones = 3 - at
    rows = jnp.where((row >= ones) & (row < ones + 3), 1.0, 0.0)
    rows = jnp.where(row == at, top, rows)
    rows = jnp.where(row == at + 1, mid, rows)
    rows = jnp.where(row == at + 2, low, rows)
    return rows.astype(jnp.bfloat16)


def eye_mask(width):
    shape = (8, width)
    return lax.broadcasted_iota(jnp.int32, shape, 0) == lax.broadcasted_iota(jnp.int32, shape, 1)


def to_row(column, width):
    return jnp.sum(jnp.where(eye_mask(width), column, 0.0), axis=0, keepdims=True)


def to_column(row):
    return jnp.sum(jnp.where(eye_mask(row.shape[1]), row, 0.0), axis=1, keepdims=True)


def kernel(
    n,
    keep,
    points_ref,
    landmarks_ref,
    chol_hbm,
    ridge_ref,
    residual_ref,
    direction_ref,
    rz_ref,
    image_out,
    direction_out,
    inner_out,
    alpha_out,
    chol,
    chol_parts,
    inverse_parts,
    inverse,
    points,
    own_aug,
    side_aug,
    col_aug,
    cross,
    kernel_store,
    rs_send,
    rs_recv,
    ag,
    proj,
    work,
    dirs,
    acc,
    side_recv,
    img_send,
    img_recv,
    curv_buf,
    chol_sem,
    rs_sems,
    ag_sems,
    dir_sems,
    curv_sems,
    img_sems,
    side_sems,
    point_recv,
    point_fwd,
    own_sems,
    share_sems,
):
    me = lax.axis_index("rows")
    feat, local = points_ref.shape
    land = landmarks_ref.shape[1]
    outs = residual_ref.shape[0]
    chips = n // 2
    half = chips // 2
    core = me % 2
    chip = me // 2
    odd = chip % 2
    pos = (1 - odd) * (chip // 2) + odd * (chips - (chip + 1) // 2)
    scale = math.log2(math.e) / feat

    def row_of(position, lane):
        position = (position + chips) % chips
        upper = position // half
        at = (1 - upper) * (2 * position) + upper * (2 * chips - 1 - 2 * position)
        return at * 2 + (core + lane) % 2

    def remote(src, dst, send, recv, to):
        return pltpu.make_async_remote_copy(
            src_ref=src,
            dst_ref=dst,
            send_sem=send,
            recv_sem=recv,
            device_id={"rows": to},
            device_id_type=pl.DeviceIdType.MESH,
        )

    def others(body):
        lax.fori_loop(1, n, lambda k, carry: (body((me + k) % n), carry)[1], 0)

    def send_all(src_of, buf, sems):
        others(lambda to: remote(src_of(to), buf.at[me], sems.at[0, to], sems.at[1, me], to).start())

    def wait_all(src_of, buf, sems):
        others(lambda to: remote(src_of(to), buf.at[to], sems.at[0, to], sems.at[1, to], to).wait_recv())

    def drain(src_of, buf, sems):
        others(lambda to: remote(src_of(to), buf.at[me], sems.at[0, to], sems.at[1, me], to).wait_send())

    chol_copy = pltpu.make_async_copy(chol_hbm, chol, chol_sem)
    chol_copy.start()

    barrier = pltpu.get_barrier_semaphore()
    others(lambda to: pl.semaphore_signal(
        barrier, inc=1, device_id={"rows": to}, device_id_type=pl.DeviceIdType.MESH))

    upper = pos // half
    partner = row_of(pos, 1)
    left = row_of(pos - 1, 0)
    left_last = row_of(pos - 1, ((pos - 1 + chips) % chips) // half)
    across = row_of(pos + half, upper)
    taker = row_of(pos + half, 1 - upper)

    def near(k):
        return row_of(pos + k, 0)

    def back(k):
        return row_of(pos - k, 0)

    def hop(k, src, owner, to):
        return remote(src, points.at[owner], point_fwd.at[k], point_recv.at[owner], to)

    own_left = hop(0, points_ref, me, left if half > 1 else left_last)
    own_side = remote(points_ref, points.at[me], own_sems.at[0], point_recv.at[me], partner)

    own_aug[0:feat, :] = points_ref[...]
    own_aug[feat:, :] = norm_rows(points_ref[...], True)
    col_aug[0:feat, :] = landmarks_ref[...]
    col_aug[feat:, :] = norm_rows(landmarks_ref[...], False)

    def entries(left_aug, at, right_aug):
        return jnp.exp2(dot_tn(left_aug[:, pl.ds(at, CHUNK)], right_aug[...]) * scale)

    proj[...] = jnp.zeros_like(proj)

    def project(i, carry):
        at = pl.multiple_of(i * CHUNK, CHUNK)
        store_split(cross, (pl.ds(at, CHUNK), slice(None)), entries(own_aug, at, col_aug))
        parts = [cross[term, pl.ds(at, CHUNK), :] for term in range(3)]
        proj[...] += dot_split(residual_ref[:, pl.ds(at, CHUNK)], parts, dot_nn)
        return carry

    lax.fori_loop(0, local // CHUNK, project, 0)
    own_square = to_row(jnp.sum(residual_ref[...] * residual_ref[...], axis=1, keepdims=True), TILE)

    pl.semaphore_wait(barrier, n - 1)

    tiles = land // TILE
    groups = land // GROUP
    rows_per = outs * tiles // n
    for piece in range(n):
        h, j = piece // tiles, piece % tiles
        rs_send[piece, 0:rows_per] = proj[h * rows_per:(h + 1) * rows_per, j * TILE:(j + 1) * TILE]
        rs_send[piece, rows_per:rows_per + 1] = own_square
    send_all(lambda to: rs_send.at[to], rs_recv, rs_sems)
    rs_recv[me, 0:rows_per + 1] = rs_send[me, 0:rows_per + 1]
    own_left.start()
    own_side.start()

    def make_left(owner_points):
        col_aug[0:feat, :] = owner_points[...]
        col_aug[feat:, :] = norm_rows(owner_points[...], False)

    def make_block(slot, right_aug):
        for at in range(0, local, CHUNK):
            kernel_store[slot, at:at + CHUNK, :] = entries(col_aug, at, right_aug).astype(jnp.bfloat16)

    chol_copy.wait()

    row = lax.broadcasted_iota(jnp.int32, (TILE, TILE), 0)
    col = lax.broadcasted_iota(jnp.int32, (TILE, TILE), 1)

    share = tiles // 2
    first = core * share

    def own_block(b):
        at = pl.multiple_of((first + b) * TILE, TILE)
        return chol[pl.ds(at, TILE), pl.ds(at, TILE)]

    inverted = [jnp.where(row == col, 1.0 / own_block(b), 0.0) for b in range(share)]
    size = 1
    while size < TILE:
        below = (row // size == col // size + 1) & (row // (2 * size) == col // (2 * size))
        for b in range(share):
            off = jnp.where(below, own_block(b), 0.0)
            if size == 1:
                on_row = jnp.sum(inverted[b], axis=1, keepdims=True)
                on_col = jnp.sum(inverted[b], axis=0, keepdims=True)
                change = on_row * off * on_col
            else:
                change = dot_nn(dot_nn(inverted[b], off, HIGH), inverted[b], HIGH)
            inverted[b] = inverted[b] - change
        size *= 2
    for b in range(share):
        inverse[first + b] = inverted[b]

    shares = inverse.at[pl.ds(first, share)]
    shared = remote(shares, shares, share_sems.at[0], share_sems.at[1], partner)
    shared.start()

    def pass_on(k):
        owner = near(k)
        to = left_last if k == half - 1 else left
        hop(k, points.at[owner], owner, left).wait_recv()
        hop(k, points.at[owner], owner, to).start()

    def pass_on_any(k):
        owner = near(k)
        hop(k, points.at[owner], owner, left).wait_recv()

        @pl.when(k < half - 1)
        def _():
            hop(k, points.at[owner], owner, left).start()

        @pl.when(k == half - 1)
        def _():
            hop(k, points.at[owner], owner, left_last).start()

    own_slot, side_slot, across_slot = 2 * half - 1, 2 * half, 2 * half - 2

    if keep:
        make_left(points_ref)
        make_block(own_slot, own_aug)
    remote(points_ref, points.at[partner], own_sems.at[0], point_recv.at[partner], partner).wait_recv()
    side_aug[0:feat, :] = points[partner]
    side_aug[feat:, :] = norm_rows(points[partner], True)
    wait_all(lambda to: rs_send.at[to], rs_recv, rs_sems)
    gathered = jnp.sum(rs_recv[:, 0:rows_per + 1], axis=0)
    ag[me] = gathered[0:rows_per]
    square = to_column(gathered[rows_per:rows_per + 1])
    send_all(lambda to: ag.at[me], ag, ag_sems)
    if half > 1:
        pass_on(1)

    other = inverse.at[pl.ds(share - first, share)]
    remote(other, other, share_sems.at[0], share_sems.at[1], partner).wait_recv()
    for b in range(groups):
        upper_block, lower_block = inverse[2 * b], inverse[2 * b + 1]
        at, end = b * GROUP, (b + 1) * GROUP
        off = chol[at + TILE:end, at:at + TILE]
        change = dot_nn(dot_nn(lower_block, off, HIGH), upper_block, HIGH)
        zero = jnp.zeros_like(upper_block)
        whole = jnp.concatenate(
            [jnp.concatenate([upper_block, zero], axis=1), jnp.concatenate([-change, lower_block], axis=1)], axis=0
        )
        store_split(inverse_parts, (b,), whole)
        if b > 0:
            store_split(chol_parts, (slice(at, end), slice(0, at)), chol[at:end, :at])

    def make_pair(k, slot):
        make_left(points.at[near(k)])
        make_block(slot, own_aug)
        make_block(slot + 1, side_aug)

    if keep:
        make_left(points.at[partner])
        make_block(side_slot, own_aug)
        if half > 1:
            make_pair(1, 0)
    wait_all(lambda to: ag.at[me], ag, ag_sems)
    for piece in range(n):
        h, j = piece // tiles, piece % tiles
        work[h * rows_per:(h + 1) * rows_per, j * TILE:(j + 1) * TILE] = ag[piece]
    pieces = [work[:, b * GROUP:(b + 1) * GROUP] for b in range(groups)]

    def block_parts(i, j):
        rows, cols = slice(i * GROUP, (i + 1) * GROUP), slice(j * GROUP, (j + 1) * GROUP)
        return [chol_parts[term, rows, cols] for term in range(3)]

    def inverse_of(b):
        return [inverse_parts[term, b] for term in range(3)]

    for b in range(groups):
        pieces[b] = dot_split(pieces[b], inverse_of(b), dot_nt)
        for i in range(b + 1, groups):
            pieces[i] = pieces[i] - dot_split(pieces[b], block_parts(i, b), dot_nt)
    halfway = jnp.concatenate(pieces, axis=1)
    if half > 2:
        pass_on(2)
    for b in reversed(range(groups)):
        pieces[b] = dot_split(pieces[b], inverse_of(b), dot_nn)
        for j in reversed(range(b)):
            pieces[j] = pieces[j] - dot_split(pieces[b], block_parts(b, j), dot_nn)
    coeffs = jnp.concatenate(pieces, axis=1)

    ridge = ridge_ref[0]
    inner = (square - jnp.sum(halfway * halfway, axis=1, keepdims=True)) / ridge
    inner_out[...] = to_row(inner, TILE)[:, :outs]
    residual = residual_ref[...]
    precond = (residual - dot_split(coeffs, [cross.at[term][...] for term in range(3)], dot_nt)) / ridge
    direction_new = precond + (inner / to_column(rz_ref[...])) * direction_ref[...]
    direction_out[...] = direction_new
    dirs[me] = direction_new.astype(jnp.bfloat16)

    def dir_to(to):
        return remote(dirs.at[me], dirs.at[to], dir_sems.at[0, to], dir_sems.at[1, me], to)

    def send_dir(to):
        remote(dirs.at[me], dirs.at[me], dir_sems.at[0, to], dir_sems.at[1, me], to).start()

    def wait_dir(src):
        remote(dirs.at[me], dirs.at[src], dir_sems.at[0, src], dir_sems.at[1, src], src).wait_recv()

    send_dir(taker)
    lax.fori_loop(1, half, lambda k, carry: (send_dir(back(half - k)), carry)[1], 0)
    send_dir(partner)
    if keep and half > 3:
        pass_on(3)

    def wait_across():
        hop(0, points.at[across], across, left).wait_recv()

    acc[...] = jnp.zeros_like(acc)

    def forward(owner, slot, side):
        acc[1] += dot_nn(dirs[owner], kernel_store[slot])
        if side:
            acc[2] += dot_nn(dirs[owner], kernel_store[slot + 1])

    def image_to(k, owner):
        return remote(img_send.at[k], img_recv.at[k], img_sems.at[0, k], img_sems.at[1, k], owner)

    def backward(k, owner, slot, side):
        total = dot_nt(dirs[me], kernel_store[slot])
        if side:
            total = total + dot_nt(dirs[partner], kernel_store[slot + 1])
        img_send[k] = total
        image_to(k, owner).start()
        wait_dir(owner)
        acc[3] += total * dirs[owner].astype(jnp.float32)

    def at_own(slot):
        acc[0] += dot_nn(dirs[me], kernel_store[slot])

    def at_side(slot):
        acc[0] += dot_nn(dirs[partner], kernel_store[slot])

    if keep:
        for k in range(2, half):
            if k > 3:
                pass_on(k)
            make_pair(k, 2 * (k - 1))
            if k == 2:
                wait_dir(partner)
            backward(k - 1, near(k), 2 * (k - 1), True)
        if half < 3:
            wait_dir(partner)
        wait_across()
        make_left(points.at[across])
        make_block(across_slot, own_aug)
        backward(half - 1, across, across_slot, False)
        if half > 1:
            backward(0, near(1), 0, True)
        at_own(own_slot)
        at_side(side_slot)
    else:
        make_left(points_ref)
        make_block(0, own_aug)
        at_own(0)
        make_left(points.at[partner])
        make_block(0, own_aug)
        wait_dir(partner)
        at_side(0)

        def both(k, carry):
            @pl.when(k > 2)
            def _():
                pass_on_any(k)

            make_pair(k, 0)
            backward(k - 1, near(k), 0, True)
            forward(near(k), 0, True)
            return carry

        lax.fori_loop(1, half, both, 0)
        wait_across()
        make_left(points.at[across])
        make_block(0, own_aug)
        backward(half - 1, across, 0, False)
        forward(across, 0, False)

    direction_new = direction_out[...]
    own_terms = direction_new * (acc[0] + ridge * direction_new) + 2.0 * acc[3]
    curv_buf[me] = to_row(jnp.sum(own_terms, axis=1, keepdims=True), TILE)
    send_all(lambda to: curv_buf.at[me], curv_buf, curv_sems)

    if keep:
        def ahead(k, carry):
            forward(near(k), 2 * (k - 1), True)
            return carry

        lax.fori_loop(1, half, ahead, 0)

    side_send = remote(acc.at[2], side_recv, side_sems.at[0], side_sems.at[1], partner)
    side_send.start()

    if keep:
        forward(across, across_slot, False)

    drain(lambda to: rs_send.at[to], rs_recv, rs_sems)
    drain(lambda to: ag.at[me], ag, ag_sems)
    shared.wait_send()
    own_left.wait_send()
    own_side.wait_send()

    def relay_drain(k, carry):
        hop(k, points.at[near(k)], near(k), left).wait_send()
        return carry

    lax.fori_loop(1, half, relay_drain, 0)

    def dir_drain(k, carry):
        dir_to(back(k)).wait_send()
        return carry

    lax.fori_loop(1, half, dir_drain, 0)
    dir_to(taker).wait_send()
    dir_to(partner).wait_send()

    side_send.wait_recv()
    image = acc[0] + acc[1] + ridge * direction_new + side_recv[...]
    for k in range(half):
        image_to(k, across).wait_recv()
        image = image + img_recv[k]
    image_out[...] = image

    wait_all(lambda to: curv_buf.at[me], curv_buf, curv_sems)
    alpha_out[...] = inner_out[...] / jnp.sum(curv_buf[...], axis=0)[:, :outs]
    drain(lambda to: curv_buf.at[me], curv_buf, curv_sems)
    side_send.wait_send()
    for k in range(half):
        image_to(k, across).wait_send()


def finish(
    image_ref,
    direction_ref,
    inner_ref,
    alpha_ref,
    solution_ref,
    residual_ref,
    solution_out,
    residual_out,
    direction_out,
    inner_out,
):
    alpha = to_column(alpha_ref[...])
    direction = direction_ref[...]
    solution_out[...] = solution_ref[...] + alpha * direction
    residual_out[...] = residual_ref[...] - alpha * image_ref[...]
    direction_out[...] = direction
    inner_out[...] = inner_ref[...]


def solution(mesh):
    n = mesh.shape["rows"]

    def local(points, landmarks, chol, ridge, solution, residual, direction, rz_prev):
        feat, own = points.shape
        land = landmarks.shape[1]
        outs = residual.shape[0]
        keep = n <= STORED_BLOCKS
        half = n // 4
        piece = outs * land // (TILE * n)
        padded = -(-(piece + 1) // 8) * 8
        f32, bf16 = jnp.float32, jnp.bfloat16
        vmem = pl.BlockSpec(memory_space=pltpu.VMEM)
        wide = jax.ShapeDtypeStruct((outs, own), f32)
        thin = jax.ShapeDtypeStruct((1, outs), f32)
        dma = pltpu.SemaphoreType.DMA
        results = pl.pallas_call(
            functools.partial(kernel, n, keep),
            out_shape=(wide, wide, thin, thin),
            in_specs=[
                vmem,
                vmem,
                pl.BlockSpec(memory_space=pl.ANY),
                pl.BlockSpec(memory_space=pltpu.SMEM),
                vmem,
                vmem,
                vmem,
            ],
            out_specs=(vmem,) * 4,
            scratch_shapes=[
                pltpu.VMEM((land, land), f32),
                pltpu.VMEM((3, land, land), bf16),
                pltpu.VMEM((3, land // GROUP, GROUP, GROUP), bf16),
                pltpu.VMEM((land // TILE, TILE, TILE), f32),
                pltpu.VMEM((n, feat, own), bf16),
                pltpu.VMEM((feat + 16, own), bf16),
                pltpu.VMEM((feat + 16, own), bf16),
                pltpu.VMEM((feat + 16, own), bf16),
                pltpu.VMEM((3, own, land), bf16),
                pltpu.VMEM((2 * half + 1 if keep else 2, own, own), bf16),
                pltpu.VMEM((n, padded, TILE), f32),
                pltpu.VMEM((n, padded, TILE), f32),
                pltpu.VMEM((n, piece, TILE), f32),
                pltpu.VMEM((outs, land), f32),
                pltpu.VMEM((outs, land), f32),
                pltpu.VMEM((n, outs, own), bf16),
                pltpu.VMEM((4, outs, own), f32),
                pltpu.VMEM((outs, own), f32),
                pltpu.VMEM((half, outs, own), f32),
                pltpu.VMEM((half, outs, own), f32),
                pltpu.VMEM((n, 1, TILE), f32),
                dma,
                dma((2, n)),
                dma((2, n)),
                dma((2, n)),
                dma((2, n)),
                dma((2, half)),
                dma((2,)),
                dma((n,)),
                dma((half,)),
                dma((2,)),
                dma((2,)),
            ],
            compiler_params=pltpu.CompilerParams(
                collective_id=0, has_side_effects=True, vmem_limit_bytes=62 * 1024 * 1024
            ),
            name="cg_step",
        )(points, landmarks, chol, ridge, residual, direction, rz_prev.reshape(1, outs))
        results = pl.pallas_call(
            finish,
            out_shape=(wide, wide, wide, thin),
            in_specs=[vmem] * 6,
            out_specs=(vmem,) * 4,
            name="finish",
        )(*results, solution, residual)
        return (results[0], results[1], results[2], results[3].reshape(outs))

    wide_spec = P(None, ("groups", "rows"))
    in_specs = (
        wide_spec,
        P(None, "groups"),
        P("groups", None),
        P("groups"),
        wide_spec,
        wide_spec,
        wide_spec,
        P("groups"),
    )
    out_specs = (wide_spec, wide_spec, wide_spec, P("groups"))
    return jax.shard_map(local, mesh=mesh, in_specs=in_specs, out_specs=out_specs, check_vma=False)
```

```python
import functools
import math

import jax
import jax.numpy as jnp
from jax import lax
from jax.experimental import pallas as pl
from jax.experimental.pallas import tpu as pltpu
from jax.sharding import PartitionSpec as P

HIGH = lax.Precision.HIGHEST
TILE = 128
CHUNK = 256
GROUP = 2 * TILE
STORED_BLOCKS = 16


def dot_nn(left, right, precision=None):
    return lax.dot_general(
        left, right, (((1,), (0,)), ((), ())), precision=precision, preferred_element_type=jnp.float32
    )


def dot_nt(left, right, precision=None):
    return lax.dot_general(
        left, right, (((1,), (1,)), ((), ())), precision=precision, preferred_element_type=jnp.float32
    )


def dot_tn(left, right):
    return lax.dot_general(
        left, right, (((0,), (0,)), ((), ())), preferred_element_type=jnp.float32
    )


def split(values):
    top = values.astype(jnp.bfloat16).astype(jnp.float32)
    rest = values - top
    mid = rest.astype(jnp.bfloat16).astype(jnp.float32)
    return top, mid, rest - mid


def store_split(ref, at, values):
    for term, part in enumerate(split(values)):
        ref[(term,) + at] = part.astype(jnp.bfloat16)


def dot_split(left, parts, dot):
    outs = left.shape[0]
    stacked = jnp.concatenate(split(left), axis=0).astype(jnp.bfloat16)
    high = dot(stacked, parts[0])
    mid = dot(stacked[:2 * outs], parts[1])
    low = dot(stacked[:2 * outs], parts[2])
    small = low[:outs] + mid[outs:] + high[2 * outs:]
    return high[:outs] + (high[outs:2 * outs] + mid[:outs] + small)


def dot_pair(left, parts, dot):
    outs = left.shape[0]
    top = left.astype(jnp.bfloat16)
    rest = (left - top.astype(jnp.float32)).astype(jnp.bfloat16)
    high = dot(jnp.concatenate([top, rest], axis=0), parts[0])
    return high[:outs] + (high[outs:] + dot(top, parts[1]))


def norm_rows(features, first):
    wide = features.astype(jnp.float32)
    half = -0.5 * jnp.sum(wide * wide, axis=0, keepdims=True)
    top = half.astype(jnp.bfloat16).astype(jnp.float32)
    rest = half - top
    mid = rest.astype(jnp.bfloat16).astype(jnp.float32)
    low = rest - mid
    row = lax.broadcasted_iota(jnp.int32, (16, features.shape[1]), 0)
    at = 0 if first else 3
    ones = 3 - at
    rows = jnp.where((row >= ones) & (row < ones + 3), 1.0, 0.0)
    rows = jnp.where(row == at, top, rows)
    rows = jnp.where(row == at + 1, mid, rows)
    rows = jnp.where(row == at + 2, low, rows)
    return rows.astype(jnp.bfloat16)


def eye_mask(width):
    shape = (8, width)
    return lax.broadcasted_iota(jnp.int32, shape, 0) == lax.broadcasted_iota(jnp.int32, shape, 1)


def to_row(column, width):
    return jnp.sum(jnp.where(eye_mask(width), column, 0.0), axis=0, keepdims=True)


def to_column(row):
    return jnp.sum(jnp.where(eye_mask(row.shape[1]), row, 0.0), axis=1, keepdims=True)


def kernel(
    n,
    keep,
    points_ref,
    landmarks_ref,
    chol_hbm,
    ridge_ref,
    residual_ref,
    direction_ref,
    rz_ref,
    image_out,
    direction_out,
    inner_out,
    alpha_out,
    chol,
    chol_parts,
    inverse_parts,
    inverse,
    points,
    own_aug,
    side_aug,
    col_aug,
    cross,
    kernel_store,
    rs_send,
    rs_recv,
    ag,
    proj,
    work,
    dirs,
    acc,
    side_recv,
    img_send,
    img_recv,
    curv_buf,
    chol_sem,
    rs_sems,
    ag_sems,
    dir_sems,
    curv_sems,
    img_sems,
    side_sems,
    point_recv,
    point_fwd,
    own_sems,
    share_sems,
):
    me = lax.axis_index("rows")
    feat, local = points_ref.shape
    land = landmarks_ref.shape[1]
    outs = residual_ref.shape[0]
    chips = n // 2
    half = chips // 2
    core = me % 2
    chip = me // 2
    odd = chip % 2
    pos = (1 - odd) * (chip // 2) + odd * (chips - (chip + 1) // 2)
    scale = math.log2(math.e) / feat

    def row_of(position, lane):
        position = (position + chips) % chips
        upper = position // half
        at = (1 - upper) * (2 * position) + upper * (2 * chips - 1 - 2 * position)
        return at * 2 + (core + lane) % 2

    def remote(src, dst, send, recv, to):
        return pltpu.make_async_remote_copy(
            src_ref=src,
            dst_ref=dst,
            send_sem=send,
            recv_sem=recv,
            device_id={"rows": to},
            device_id_type=pl.DeviceIdType.MESH,
        )

    def others(body):
        lax.fori_loop(1, n, lambda k, carry: (body((me + k) % n), carry)[1], 0)

    def send_all(src_of, buf, sems):
        others(lambda to: remote(src_of(to), buf.at[me], sems.at[0, to], sems.at[1, me], to).start())

    def wait_all(src_of, buf, sems):
        others(lambda to: remote(src_of(to), buf.at[to], sems.at[0, to], sems.at[1, to], to).wait_recv())

    def drain(src_of, buf, sems):
        others(lambda to: remote(src_of(to), buf.at[me], sems.at[0, to], sems.at[1, me], to).wait_send())

    chol_copy = pltpu.make_async_copy(chol_hbm, chol, chol_sem)
    chol_copy.start()

    barrier = pltpu.get_barrier_semaphore()
    others(lambda to: pl.semaphore_signal(
        barrier, inc=1, device_id={"rows": to}, device_id_type=pl.DeviceIdType.MESH))

    upper = pos // half
    partner = row_of(pos, 1)
    left = row_of(pos - 1, 0)
    left_last = row_of(pos - 1, ((pos - 1 + chips) % chips) // half)
    across = row_of(pos + half, upper)
    taker = row_of(pos + half, 1 - upper)

    def near(k):
        return row_of(pos + k, 0)

    def back(k):
        return row_of(pos - k, 0)

    def hop(k, src, owner, to):
        return remote(src, points.at[owner], point_fwd.at[k], point_recv.at[owner], to)

    own_left = hop(0, points_ref, me, left if half > 1 else left_last)
    own_side = remote(points_ref, points.at[me], own_sems.at[0], point_recv.at[me], partner)

    own_aug[0:feat, :] = points_ref[...]
    own_aug[feat:, :] = norm_rows(points_ref[...], True)
    col_aug[0:feat, :] = landmarks_ref[...]
    col_aug[feat:, :] = norm_rows(landmarks_ref[...], False)

    def entries(left_aug, at, right_aug):
        return jnp.exp2(dot_tn(left_aug[:, pl.ds(at, CHUNK)], right_aug[...]) * scale)

    proj[...] = jnp.zeros_like(proj)

    def project(i, carry):
        at = pl.multiple_of(i * CHUNK, CHUNK)
        values = entries(own_aug, at, col_aug)
        top = values.astype(jnp.bfloat16)
        cross[0, pl.ds(at, CHUNK), :] = top
        cross[1, pl.ds(at, CHUNK), :] = (values - top.astype(jnp.float32)).astype(jnp.bfloat16)
        parts = [cross[term, pl.ds(at, CHUNK), :] for term in range(2)]
        proj[...] += dot_pair(residual_ref[:, pl.ds(at, CHUNK)], parts, dot_nn)
        return carry

    lax.fori_loop(0, local // CHUNK, project, 0)
    own_square = to_row(jnp.sum(residual_ref[...] * residual_ref[...], axis=1, keepdims=True), TILE)

    pl.semaphore_wait(barrier, n - 1)

    tiles = land // TILE
    groups = land // GROUP
    rows_per = outs * tiles // n
    for piece in range(n):
        h, j = piece // tiles, piece % tiles
        rs_send[piece, 0:rows_per] = proj[h * rows_per:(h + 1) * rows_per, j * TILE:(j + 1) * TILE]
        rs_send[piece, rows_per:rows_per + 1] = own_square
    send_all(lambda to: rs_send.at[to], rs_recv, rs_sems)
    rs_recv[me, 0:rows_per + 1] = rs_send[me, 0:rows_per + 1]
    own_left.start()
    own_side.start()

    def make_left(owner_points):
        col_aug[0:feat, :] = owner_points[...]
        col_aug[feat:, :] = norm_rows(owner_points[...], False)

    def make_block(slot, right_aug):
        for at in range(0, local, CHUNK):
            kernel_store[slot, at:at + CHUNK, :] = entries(col_aug, at, right_aug).astype(jnp.bfloat16)

    chol_copy.wait()

    row = lax.broadcasted_iota(jnp.int32, (TILE, TILE), 0)
    col = lax.broadcasted_iota(jnp.int32, (TILE, TILE), 1)

    share = tiles // 2
    first = core * share

    def own_block(b):
        at = pl.multiple_of((first + b) * TILE, TILE)
        return chol[pl.ds(at, TILE), pl.ds(at, TILE)]

    inverted = [jnp.where(row == col, 1.0 / own_block(b), 0.0) for b in range(share)]
    size = 1
    while size < TILE:
        below = (row // size == col // size + 1) & (row // (2 * size) == col // (2 * size))
        for b in range(share):
            off = jnp.where(below, own_block(b), 0.0)
            if size == 1:
                on_row = jnp.sum(inverted[b], axis=1, keepdims=True)
                on_col = jnp.sum(inverted[b], axis=0, keepdims=True)
                change = on_row * off * on_col
            else:
                change = dot_nn(dot_nn(inverted[b], off, HIGH), inverted[b], HIGH)
            inverted[b] = inverted[b] - change
        size *= 2
    for b in range(share):
        inverse[first + b] = inverted[b]

    shares = inverse.at[pl.ds(first, share)]
    shared = remote(shares, shares, share_sems.at[0], share_sems.at[1], partner)
    shared.start()

    def pass_on(k):
        owner = near(k)
        to = left_last if k == half - 1 else left
        hop(k, points.at[owner], owner, left).wait_recv()
        hop(k, points.at[owner], owner, to).start()

    def pass_on_any(k):
        owner = near(k)
        hop(k, points.at[owner], owner, left).wait_recv()

        @pl.when(k < half - 1)
        def _():
            hop(k, points.at[owner], owner, left).start()

        @pl.when(k == half - 1)
        def _():
            hop(k, points.at[owner], owner, left_last).start()

    own_slot, side_slot, across_slot = 2 * half - 1, 2 * half, 2 * half - 2

    if keep:
        make_left(points_ref)
        make_block(own_slot, own_aug)
    remote(points_ref, points.at[partner], own_sems.at[0], point_recv.at[partner], partner).wait_recv()
    side_aug[0:feat, :] = points[partner]
    side_aug[feat:, :] = norm_rows(points[partner], True)
    wait_all(lambda to: rs_send.at[to], rs_recv, rs_sems)
    gathered = jnp.sum(rs_recv[:, 0:rows_per + 1], axis=0)
    ag[me] = gathered[0:rows_per]
    square = to_column(gathered[rows_per:rows_per + 1])
    send_all(lambda to: ag.at[me], ag, ag_sems)
    if half > 1:
        pass_on(1)

    other = inverse.at[pl.ds(share - first, share)]
    remote(other, other, share_sems.at[0], share_sems.at[1], partner).wait_recv()
    for b in range(groups):
        upper_block, lower_block = inverse[2 * b], inverse[2 * b + 1]
        at, end = b * GROUP, (b + 1) * GROUP
        off = chol[at + TILE:end, at:at + TILE]
        change = dot_nn(dot_nn(lower_block, off, HIGH), upper_block, HIGH)
        zero = jnp.zeros_like(upper_block)
        whole = jnp.concatenate(
            [jnp.concatenate([upper_block, zero], axis=1), jnp.concatenate([-change, lower_block], axis=1)], axis=0
        )
        store_split(inverse_parts, (b,), whole)
        if b > 0:
            store_split(chol_parts, (slice(at, end), slice(0, at)), chol[at:end, :at])

    def make_pair(k, slot):
        make_left(points.at[near(k)])
        make_block(slot, own_aug)
        make_block(slot + 1, side_aug)

    if keep:
        make_left(points.at[partner])
        make_block(side_slot, own_aug)
        if half > 1:
            make_pair(1, 0)
    wait_all(lambda to: ag.at[me], ag, ag_sems)
    for piece in range(n):
        h, j = piece // tiles, piece % tiles
        work[h * rows_per:(h + 1) * rows_per, j * TILE:(j + 1) * TILE] = ag[piece]
    pieces = [work[:, b * GROUP:(b + 1) * GROUP] for b in range(groups)]

    def block_parts(i, j):
        rows, cols = slice(i * GROUP, (i + 1) * GROUP), slice(j * GROUP, (j + 1) * GROUP)
        return [chol_parts[term, rows, cols] for term in range(3)]

    def inverse_of(b):
        return [inverse_parts[term, b] for term in range(3)]

    for b in range(groups):
        pieces[b] = dot_split(pieces[b], inverse_of(b), dot_nt)
        for i in range(b + 1, groups):
            pieces[i] = pieces[i] - dot_split(pieces[b], block_parts(i, b), dot_nt)
    halfway = jnp.concatenate(pieces, axis=1)
    if half > 2:
        pass_on(2)
    for b in reversed(range(groups)):
        pieces[b] = dot_split(pieces[b], inverse_of(b), dot_nn)
        for j in reversed(range(b)):
            pieces[j] = pieces[j] - dot_split(pieces[b], block_parts(b, j), dot_nn)
    coeffs = jnp.concatenate(pieces, axis=1)

    ridge = ridge_ref[...]
    inner = (square - jnp.sum(halfway * halfway, axis=1, keepdims=True)) / ridge
    inner_out[...] = to_row(inner, TILE)[:, :outs]
    residual = residual_ref[...]
    precond = (residual - dot_pair(coeffs, [cross.at[term][...] for term in range(2)], dot_nt)) / ridge
    direction_new = precond + (inner / to_column(rz_ref[...])) * direction_ref[...]
    direction_out[...] = direction_new
    dirs[me] = direction_new.astype(jnp.bfloat16)

    def dir_to(to):
        return remote(dirs.at[me], dirs.at[to], dir_sems.at[0, to], dir_sems.at[1, me], to)

    def send_dir(to):
        remote(dirs.at[me], dirs.at[me], dir_sems.at[0, to], dir_sems.at[1, me], to).start()

    def wait_dir(src):
        remote(dirs.at[me], dirs.at[src], dir_sems.at[0, src], dir_sems.at[1, src], src).wait_recv()

    send_dir(taker)
    lax.fori_loop(1, half, lambda k, carry: (send_dir(back(half - k)), carry)[1], 0)
    send_dir(partner)
    if keep and half > 3:
        pass_on(3)

    def wait_across():
        hop(0, points.at[across], across, left).wait_recv()

    acc[...] = jnp.zeros_like(acc)

    def forward(owner, slot, side):
        acc[1] += dot_nn(dirs[owner], kernel_store[slot])
        if side:
            acc[2] += dot_nn(dirs[owner], kernel_store[slot + 1])

    def image_to(k, owner):
        return remote(img_send.at[k], img_recv.at[k], img_sems.at[0, k], img_sems.at[1, k], owner)

    def backward(k, owner, slot, side):
        total = dot_nt(dirs[me], kernel_store[slot])
        if side:
            total = total + dot_nt(dirs[partner], kernel_store[slot + 1])
        img_send[k] = total
        image_to(k, owner).start()
        return total

    def at_own(slot):
        acc[0] += dot_nn(dirs[me], kernel_store[slot])

    def at_side(slot):
        acc[0] += dot_nn(dirs[partner], kernel_store[slot])

    early = 3

    def terms_behind(total, owner):
        acc[3] += total * dirs[owner].astype(jnp.float32)

    if keep:
        for k in range(2, half):
            if k > 3:
                pass_on(k)
            make_pair(k, 2 * (k - 1))
            if k == 2:
                wait_dir(partner)
            if k >= early:
                sent = backward(k - 1, near(k), 2 * (k - 1), True)
                wait_dir(near(k))
                terms_behind(sent, near(k))
        if half < 3:
            wait_dir(partner)
        wait_across()
        make_left(points.at[across])
        make_block(across_slot, own_aug)
        sent = backward(half - 1, across, across_slot, False)
        at_own(own_slot)
        at_side(side_slot)
        wait_dir(across)
        terms_behind(sent, across)

        def ahead(k, carry):
            wait_dir(near(k))
            forward(near(k), 2 * (k - 1), True)
            return carry

        lax.fori_loop(1, min(half, early), ahead, 0)
        low = dirs[partner].astype(jnp.float32)
        acc[3] += direction_out[...] * acc[1] + low * acc[2]
    else:
        make_left(points_ref)
        make_block(0, own_aug)
        at_own(0)
        make_left(points.at[partner])
        make_block(0, own_aug)
        wait_dir(partner)
        at_side(0)

        def both(k, carry):
            @pl.when(k > 2)
            def _():
                pass_on_any(k)

            make_pair(k, 0)
            backward(k - 1, near(k), 0, True)
            wait_dir(near(k))
            forward(near(k), 0, True)
            return carry

        lax.fori_loop(1, half, both, 0)
        wait_across()
        make_left(points.at[across])
        make_block(0, own_aug)
        backward(half - 1, across, 0, False)
        wait_dir(across)
        forward(across, 0, False)
        low = dirs[partner].astype(jnp.float32)
        acc[3] = direction_out[...] * acc[1] + low * acc[2]

    direction_new = direction_out[...]
    own_terms = direction_new * (acc[0] + ridge * direction_new) + 2.0 * acc[3]
    curv_buf[me] = to_row(jnp.sum(own_terms, axis=1, keepdims=True), TILE)
    send_all(lambda to: curv_buf.at[me], curv_buf, curv_sems)

    if keep:
        last = min(half, early)

        def behind(i, carry):
            k = last - i
            backward(k - 1, near(k), 2 * (k - 1), True)
            return carry

        lax.fori_loop(1, last, behind, 0)
        for k in range(early, half):
            forward(near(k), 2 * (k - 1), True)

    side_send = remote(acc.at[2], side_recv, side_sems.at[0], side_sems.at[1], partner)
    side_send.start()

    if keep:
        forward(across, across_slot, False)

    drain(lambda to: rs_send.at[to], rs_recv, rs_sems)
    drain(lambda to: ag.at[me], ag, ag_sems)
    shared.wait_send()
    own_left.wait_send()
    own_side.wait_send()

    def relay_drain(k, carry):
        hop(k, points.at[near(k)], near(k), left).wait_send()
        return carry

    lax.fori_loop(1, half, relay_drain, 0)

    def dir_drain(k, carry):
        dir_to(back(k)).wait_send()
        return carry

    lax.fori_loop(1, half, dir_drain, 0)
    dir_to(taker).wait_send()
    dir_to(partner).wait_send()

    side_send.wait_recv()
    image = acc[0] + acc[1] + ridge * direction_new + side_recv[...]
    for k in range(half):
        image_to(k, across).wait_recv()
        image = image + img_recv[k]
    image_out[...] = image

    wait_all(lambda to: curv_buf.at[me], curv_buf, curv_sems)
    alpha_out[...] = inner_out[...] / jnp.sum(curv_buf[...], axis=0)[:, :outs]
    drain(lambda to: curv_buf.at[me], curv_buf, curv_sems)
    side_send.wait_send()
    for k in range(half):
        image_to(k, across).wait_send()


def finish(
    image_ref,
    direction_ref,
    inner_ref,
    alpha_ref,
    solution_ref,
    residual_ref,
    solution_out,
    residual_out,
    direction_out,
    inner_out,
):
    alpha = to_column(alpha_ref[...])
    direction = direction_ref[...]
    solution_out[...] = solution_ref[...] + alpha * direction
    residual_out[...] = residual_ref[...] - alpha * image_ref[...]
    direction_out[...] = direction
    inner_out[...] = inner_ref[...]


def solution(mesh):
    n = mesh.shape["rows"]

    def local(points, landmarks, chol, ridge, solution, residual, direction, rz_prev):
        feat, own = points.shape
        land = landmarks.shape[1]
        outs = residual.shape[0]
        keep = n <= STORED_BLOCKS
        half = n // 4
        piece = outs * land // (TILE * n)
        padded = -(-(piece + 1) // 8) * 8
        f32, bf16 = jnp.float32, jnp.bfloat16
        vmem = pl.BlockSpec(memory_space=pltpu.VMEM)
        wide = jax.ShapeDtypeStruct((outs, own), f32)
        thin = jax.ShapeDtypeStruct((1, outs), f32)
        dma = pltpu.SemaphoreType.DMA
        results = pl.pallas_call(
            functools.partial(kernel, n, keep),
            out_shape=(wide, wide, thin, thin),
            in_specs=[
                vmem,
                vmem,
                pl.BlockSpec(memory_space=pl.ANY),
                vmem,
                vmem,
                vmem,
                vmem,
            ],
            out_specs=(vmem,) * 4,
            scratch_shapes=[
                pltpu.VMEM((land, land), f32),
                pltpu.VMEM((3, land, land), bf16),
                pltpu.VMEM((3, land // GROUP, GROUP, GROUP), bf16),
                pltpu.VMEM((land // TILE, TILE, TILE), f32),
                pltpu.VMEM((n, feat, own), bf16),
                pltpu.VMEM((feat + 16, own), bf16),
                pltpu.VMEM((feat + 16, own), bf16),
                pltpu.VMEM((feat + 16, own), bf16),
                pltpu.VMEM((2, own, land), bf16),
                pltpu.VMEM((2 * half + 1 if keep else 2, own, own), bf16),
                pltpu.VMEM((n, padded, TILE), f32),
                pltpu.VMEM((n, padded, TILE), f32),
                pltpu.VMEM((n, piece, TILE), f32),
                pltpu.VMEM((outs, land), f32),
                pltpu.VMEM((outs, land), f32),
                pltpu.VMEM((n, outs, own), bf16),
                pltpu.VMEM((4, outs, own), f32),
                pltpu.VMEM((outs, own), f32),
                pltpu.VMEM((half, outs, own), f32),
                pltpu.VMEM((half, outs, own), f32),
                pltpu.VMEM((n, 1, TILE), f32),
                dma,
                dma((2, n)),
                dma((2, n)),
                dma((2, n)),
                dma((2, n)),
                dma((2, half)),
                dma((2,)),
                dma((n,)),
                dma((half,)),
                dma((2,)),
                dma((2,)),
            ],
            compiler_params=pltpu.CompilerParams(
                collective_id=0, has_side_effects=True, vmem_limit_bytes=62 * 1024 * 1024
            ),
            name="cg_step",
        )(points, landmarks, chol, ridge.reshape(1, 1), residual, direction, rz_prev.reshape(1, outs))
        results = pl.pallas_call(
            finish,
            out_shape=(wide, wide, wide, thin),
            in_specs=[vmem] * 6,
            out_specs=(vmem,) * 4,
            name="finish",
        )(*results, solution, residual)
        return (results[0], results[1], results[2], results[3].reshape(outs))

    wide_spec = P(None, ("groups", "rows"))
    in_specs = (
        wide_spec,
        P(None, "groups"),
        P("groups", None),
        P("groups"),
        wide_spec,
        wide_spec,
        wide_spec,
        P("groups"),
    )
    out_specs = (wide_spec, wide_spec, wide_spec, P("groups"))
    return jax.shard_map(local, mesh=mesh, in_specs=in_specs, out_specs=out_specs, check_vma=False)
```

```python
import functools
import math

import jax
import jax.numpy as jnp
from jax import lax
from jax.experimental import pallas as pl
from jax.experimental.pallas import tpu as pltpu
from jax.sharding import PartitionSpec as P

HIGH = lax.Precision.HIGHEST
TILE = 128
CHUNK = 256
GROUP = 2 * TILE
STORED_BLOCKS = 16


def dot_nn(left, right, precision=None):
    return lax.dot_general(
        left, right, (((1,), (0,)), ((), ())), precision=precision, preferred_element_type=jnp.float32
    )


def dot_nt(left, right, precision=None):
    return lax.dot_general(
        left, right, (((1,), (1,)), ((), ())), precision=precision, preferred_element_type=jnp.float32
    )


def dot_tn(left, right):
    return lax.dot_general(
        left, right, (((0,), (0,)), ((), ())), preferred_element_type=jnp.float32
    )


def split(values):
    top = values.astype(jnp.bfloat16).astype(jnp.float32)
    rest = values - top
    mid = rest.astype(jnp.bfloat16).astype(jnp.float32)
    return top, mid, rest - mid


def store_split(ref, at, values):
    for term, part in enumerate(split(values)):
        ref[(term,) + at] = part.astype(jnp.bfloat16)


def dot_split(left, parts, dot):
    outs = left.shape[0]
    stacked = jnp.concatenate(split(left), axis=0).astype(jnp.bfloat16)
    high = dot(stacked, parts[0])
    mid = dot(stacked[:2 * outs], parts[1])
    low = dot(stacked[:2 * outs], parts[2])
    small = low[:outs] + mid[outs:] + high[2 * outs:]
    return high[:outs] + (high[outs:2 * outs] + mid[:outs] + small)


def dot_pair(left, parts, dot):
    outs = left.shape[0]
    top = left.astype(jnp.bfloat16)
    rest = (left - top.astype(jnp.float32)).astype(jnp.bfloat16)
    high = dot(jnp.concatenate([top, rest], axis=0), parts[0])
    return high[:outs] + (high[outs:] + dot(top, parts[1]))


def norm_rows(features, first):
    wide = features.astype(jnp.float32)
    half = -0.5 * jnp.sum(wide * wide, axis=0, keepdims=True)
    top = half.astype(jnp.bfloat16).astype(jnp.float32)
    rest = half - top
    mid = rest.astype(jnp.bfloat16).astype(jnp.float32)
    low = rest - mid
    row = lax.broadcasted_iota(jnp.int32, (16, features.shape[1]), 0)
    at = 0 if first else 3
    ones = 3 - at
    rows = jnp.where((row >= ones) & (row < ones + 3), 1.0, 0.0)
    rows = jnp.where(row == at, top, rows)
    rows = jnp.where(row == at + 1, mid, rows)
    rows = jnp.where(row == at + 2, low, rows)
    return rows.astype(jnp.bfloat16)


def eye_mask(width):
    shape = (8, width)
    return lax.broadcasted_iota(jnp.int32, shape, 0) == lax.broadcasted_iota(jnp.int32, shape, 1)


def to_row(column, width):
    return jnp.sum(jnp.where(eye_mask(width), column, 0.0), axis=0, keepdims=True)


def to_column(row):
    return jnp.sum(jnp.where(eye_mask(row.shape[1]), row, 0.0), axis=1, keepdims=True)


def kernel(
    n,
    keep,
    points_ref,
    landmarks_ref,
    chol_hbm,
    ridge_ref,
    residual_ref,
    direction_ref,
    rz_ref,
    image_out,
    direction_out,
    inner_out,
    alpha_out,
    chol,
    chol_parts,
    inverse_parts,
    inverse,
    points,
    own_aug,
    side_aug,
    col_aug,
    cross,
    kernel_store,
    rs_send,
    rs_recv,
    ag,
    proj,
    work,
    dirs,
    acc,
    side_recv,
    img_send,
    img_recv,
    curv_buf,
    chol_sem,
    rs_sems,
    ag_sems,
    dir_sems,
    curv_sems,
    img_sems,
    side_sems,
    point_recv,
    point_fwd,
    own_sems,
    share_sems,
):
    me = lax.axis_index("rows")
    feat, local = points_ref.shape
    land = landmarks_ref.shape[1]
    outs = residual_ref.shape[0]
    chips = n // 2
    half = chips // 2
    core = me % 2
    chip = me // 2
    odd = chip % 2
    pos = (1 - odd) * (chip // 2) + odd * (chips - (chip + 1) // 2)
    scale = math.log2(math.e) / feat

    def row_of(position, lane):
        position = (position + chips) % chips
        upper = position // half
        at = (1 - upper) * (2 * position) + upper * (2 * chips - 1 - 2 * position)
        return at * 2 + (core + lane) % 2

    def remote(src, dst, send, recv, to):
        return pltpu.make_async_remote_copy(
            src_ref=src,
            dst_ref=dst,
            send_sem=send,
            recv_sem=recv,
            device_id={"rows": to},
            device_id_type=pl.DeviceIdType.MESH,
        )

    def others(body):
        lax.fori_loop(1, n, lambda k, carry: (body((me + k) % n), carry)[1], 0)

    def send_all(src_of, buf, sems):
        others(lambda to: remote(src_of(to), buf.at[me], sems.at[0, to], sems.at[1, me], to).start())

    def wait_all(src_of, buf, sems):
        others(lambda to: remote(src_of(to), buf.at[to], sems.at[0, to], sems.at[1, to], to).wait_recv())

    def drain(src_of, buf, sems):
        others(lambda to: remote(src_of(to), buf.at[me], sems.at[0, to], sems.at[1, me], to).wait_send())

    chol_copy = pltpu.make_async_copy(chol_hbm, chol, chol_sem)
    chol_copy.start()

    barrier = pltpu.get_barrier_semaphore()
    others(lambda to: pl.semaphore_signal(
        barrier, inc=1, device_id={"rows": to}, device_id_type=pl.DeviceIdType.MESH))

    upper = pos // half
    partner = row_of(pos, 1)
    left = row_of(pos - 1, 0)
    left_last = row_of(pos - 1, ((pos - 1 + chips) % chips) // half)
    across = row_of(pos + half, upper)
    taker = row_of(pos + half, 1 - upper)

    def near(k):
        return row_of(pos + k, 0)

    def back(k):
        return row_of(pos - k, 0)

    def hop(k, h, src, owner, to):
        part = pl.ds(h * (feat // 2), feat // 2)
        return remote(src.at[part], points.at[owner, part], point_fwd.at[k, h], point_recv.at[owner, h], to)

    own_left = [hop(0, h, points_ref, me, left if half > 1 else left_last) for h in range(2)]
    own_side = remote(points_ref, points.at[me], own_sems.at[0], own_sems.at[1], partner)

    own_aug[0:feat, :] = points_ref[...]
    own_aug[feat:, :] = norm_rows(points_ref[...], True)
    col_aug[0:feat, :] = landmarks_ref[...]
    col_aug[feat:, :] = norm_rows(landmarks_ref[...], False)

    def entries(left_aug, at, right_aug):
        return jnp.exp2(dot_tn(left_aug[:, pl.ds(at, CHUNK)], right_aug[...]) * scale)

    proj[...] = jnp.zeros_like(proj)

    def project(i, carry):
        at = pl.multiple_of(i * CHUNK, CHUNK)
        values = entries(own_aug, at, col_aug)
        top = values.astype(jnp.bfloat16)
        cross[0, pl.ds(at, CHUNK), :] = top
        cross[1, pl.ds(at, CHUNK), :] = (values - top.astype(jnp.float32)).astype(jnp.bfloat16)
        parts = [cross[term, pl.ds(at, CHUNK), :] for term in range(2)]
        proj[...] += dot_pair(residual_ref[:, pl.ds(at, CHUNK)], parts, dot_nn)
        return carry

    lax.fori_loop(0, local // CHUNK, project, 0)
    own_square = to_row(jnp.sum(residual_ref[...] * residual_ref[...], axis=1, keepdims=True), TILE)

    pl.semaphore_wait(barrier, n - 1)

    tiles = land // TILE
    groups = land // GROUP
    rows_per = outs * tiles // n
    for piece in range(n):
        h, j = piece // tiles, piece % tiles
        rs_send[piece, 0:rows_per] = proj[h * rows_per:(h + 1) * rows_per, j * TILE:(j + 1) * TILE]
        rs_send[piece, rows_per:rows_per + 1] = own_square
    send_all(lambda to: rs_send.at[to], rs_recv, rs_sems)
    rs_recv[me, 0:rows_per + 1] = rs_send[me, 0:rows_per + 1]
    own_side.start()
    for copy in own_left:
        copy.start()

    def make_left(owner_points):
        col_aug[0:feat, :] = owner_points[...]
        col_aug[feat:, :] = norm_rows(owner_points[...], False)

    def make_block(slot, right_aug):
        for at in range(0, local, CHUNK):
            kernel_store[slot, at:at + CHUNK, :] = entries(col_aug, at, right_aug).astype(jnp.bfloat16)

    chol_copy.wait()

    row = lax.broadcasted_iota(jnp.int32, (TILE, TILE), 0)
    col = lax.broadcasted_iota(jnp.int32, (TILE, TILE), 1)

    share = tiles // 2
    first = core * share

    def own_block(b):
        at = pl.multiple_of((first + b) * TILE, TILE)
        return chol[pl.ds(at, TILE), pl.ds(at, TILE)]

    inverted = [jnp.where(row == col, 1.0 / own_block(b), 0.0) for b in range(share)]
    size = 1
    while size < TILE:
        below = (row // size == col // size + 1) & (row // (2 * size) == col // (2 * size))
        for b in range(share):
            off = jnp.where(below, own_block(b), 0.0)
            if size == 1:
                on_row = jnp.sum(inverted[b], axis=1, keepdims=True)
                on_col = jnp.sum(inverted[b], axis=0, keepdims=True)
                change = on_row * off * on_col
            else:
                change = dot_nn(dot_nn(inverted[b], off, HIGH), inverted[b], HIGH)
            inverted[b] = inverted[b] - change
        size *= 2
    for b in range(share):
        inverse[first + b] = inverted[b]

    shares = inverse.at[pl.ds(first, share)]
    shared = remote(shares, shares, share_sems.at[0], share_sems.at[1], partner)
    shared.start()

    def pass_on(k, h):
        owner = near(k)
        to = left_last if k == half - 1 else left
        hop(k, h, points.at[owner], owner, left).wait_recv()
        hop(k, h, points.at[owner], owner, to).start()

    def pass_on_any(k):
        owner = near(k)
        for h in range(2):
            hop(k, h, points.at[owner], owner, left).wait_recv()

        @pl.when(k < half - 1)
        def _():
            for h in range(2):
                hop(k, h, points.at[owner], owner, left).start()

        @pl.when(k == half - 1)
        def _():
            for h in range(2):
                hop(k, h, points.at[owner], owner, left_last).start()

    own_slot, side_slot, across_slot = 2 * half - 1, 2 * half, 2 * half - 2

    if keep:
        make_left(points_ref)
        make_block(own_slot, own_aug)
    remote(points_ref, points.at[partner], own_sems.at[0], own_sems.at[1], partner).wait_recv()
    side_aug[0:feat, :] = points[partner]
    side_aug[feat:, :] = norm_rows(points[partner], True)
    wait_all(lambda to: rs_send.at[to], rs_recv, rs_sems)
    gathered = jnp.sum(rs_recv[:, 0:rows_per + 1], axis=0)
    ag[me] = gathered[0:rows_per]
    square = to_column(gathered[rows_per:rows_per + 1])
    send_all(lambda to: ag.at[me], ag, ag_sems)
    if half > 1:
        pass_on(1, 0)

    other = inverse.at[pl.ds(share - first, share)]
    remote(other, other, share_sems.at[0], share_sems.at[1], partner).wait_recv()
    for b in range(groups):
        upper_block, lower_block = inverse[2 * b], inverse[2 * b + 1]
        at, end = b * GROUP, (b + 1) * GROUP
        off = chol[at + TILE:end, at:at + TILE]
        change = dot_nn(dot_nn(lower_block, off, HIGH), upper_block, HIGH)
        zero = jnp.zeros_like(upper_block)
        whole = jnp.concatenate(
            [jnp.concatenate([upper_block, zero], axis=1), jnp.concatenate([-change, lower_block], axis=1)], axis=0
        )
        store_split(inverse_parts, (b,), whole)
        if b > 0:
            store_split(chol_parts, (slice(at, end), slice(0, at)), chol[at:end, :at])

    def make_pair(k, slot):
        make_left(points.at[near(k)])
        make_block(slot, own_aug)
        make_block(slot + 1, side_aug)

    if half > 1:
        pass_on(1, 1)
    if keep:
        make_left(points.at[partner])
        make_block(side_slot, own_aug)
        if half > 1:
            make_pair(1, 0)
    if half > 2:
        pass_on(2, 0)
    wait_all(lambda to: ag.at[me], ag, ag_sems)
    for piece in range(n):
        h, j = piece // tiles, piece % tiles
        work[h * rows_per:(h + 1) * rows_per, j * TILE:(j + 1) * TILE] = ag[piece]
    pieces = [work[:, b * GROUP:(b + 1) * GROUP] for b in range(groups)]

    def block_parts(i, j):
        rows, cols = slice(i * GROUP, (i + 1) * GROUP), slice(j * GROUP, (j + 1) * GROUP)
        return [chol_parts[term, rows, cols] for term in range(3)]

    def inverse_of(b):
        return [inverse_parts[term, b] for term in range(3)]

    for b in range(groups):
        pieces[b] = dot_split(pieces[b], inverse_of(b), dot_nt)
        for i in range(b + 1, groups):
            pieces[i] = pieces[i] - dot_split(pieces[b], block_parts(i, b), dot_nt)
    halfway = jnp.concatenate(pieces, axis=1)
    if half > 2:
        pass_on(2, 1)
    for b in reversed(range(groups)):
        pieces[b] = dot_split(pieces[b], inverse_of(b), dot_nn)
        for j in reversed(range(b)):
            pieces[j] = pieces[j] - dot_split(pieces[b], block_parts(b, j), dot_nn)
    coeffs = jnp.concatenate(pieces, axis=1)

    ridge = ridge_ref[...]
    inner = (square - jnp.sum(halfway * halfway, axis=1, keepdims=True)) / ridge
    inner_out[...] = to_row(inner, TILE)[:, :outs]
    residual = residual_ref[...]
    precond = (residual - dot_pair(coeffs, [cross.at[term][...] for term in range(2)], dot_nt)) / ridge
    direction_new = precond + (inner / to_column(rz_ref[...])) * direction_ref[...]
    direction_out[...] = direction_new
    dirs[me] = direction_new.astype(jnp.bfloat16)

    def dir_to(to):
        return remote(dirs.at[me], dirs.at[to], dir_sems.at[0, to], dir_sems.at[1, me], to)

    def send_dir(to):
        remote(dirs.at[me], dirs.at[me], dir_sems.at[0, to], dir_sems.at[1, me], to).start()

    def wait_dir(src):
        remote(dirs.at[me], dirs.at[src], dir_sems.at[0, src], dir_sems.at[1, src], src).wait_recv()

    send_dir(taker)
    lax.fori_loop(1, half, lambda k, carry: (send_dir(back(half - k)), carry)[1], 0)
    send_dir(partner)
    if keep and half > 3:
        pass_on(3, 0)

    def wait_across():
        for h in range(2):
            hop(0, h, points.at[across], across, left).wait_recv()

    acc[...] = jnp.zeros_like(acc)

    def forward(owner, slot, side):
        acc[1] += dot_nn(dirs[owner], kernel_store[slot])
        if side:
            acc[2] += dot_nn(dirs[owner], kernel_store[slot + 1])

    def image_to(k, owner):
        return remote(img_send.at[k], img_recv.at[k], img_sems.at[0, k], img_sems.at[1, k], owner)

    def backward(k, owner, slot, side):
        total = dot_nt(dirs[me], kernel_store[slot])
        if side:
            total = total + dot_nt(dirs[partner], kernel_store[slot + 1])
        img_send[k] = total
        image_to(k, owner).start()
        return total

    def at_own(slot):
        acc[0] += dot_nn(dirs[me], kernel_store[slot])

    def at_side(slot):
        acc[0] += dot_nn(dirs[partner], kernel_store[slot])

    early = 3

    def terms_behind(total, owner):
        acc[3] += total * dirs[owner].astype(jnp.float32)

    if keep:
        for k in range(2, half):
            if k > 3:
                pass_on(k, 0)
                pass_on(k, 1)
            make_pair(k, 2 * (k - 1))
            if k == 2 and half > 3:
                pass_on(3, 1)
            if k == 2:
                wait_dir(partner)
            if k >= early:
                sent = backward(k - 1, near(k), 2 * (k - 1), True)
                wait_dir(near(k))
                terms_behind(sent, near(k))
        if half < 3:
            wait_dir(partner)
        at_own(own_slot)
        at_side(side_slot)

        def ahead(k, carry):
            wait_dir(near(k))
            forward(near(k), 2 * (k - 1), True)
            return carry

        lax.fori_loop(1, min(half, early), ahead, 0)
        low = dirs[partner].astype(jnp.float32)
        acc[3] += direction_out[...] * acc[1] + low * acc[2]
        wait_across()
        make_left(points.at[across])
        make_block(across_slot, own_aug)
        sent = backward(half - 1, across, across_slot, False)
        wait_dir(across)
        terms_behind(sent, across)
    else:
        make_left(points_ref)
        make_block(0, own_aug)
        at_own(0)
        make_left(points.at[partner])
        make_block(0, own_aug)
        wait_dir(partner)
        at_side(0)

        def both(k, carry):
            @pl.when(k > 2)
            def _():
                pass_on_any(k)

            make_pair(k, 0)
            backward(k - 1, near(k), 0, True)
            wait_dir(near(k))
            forward(near(k), 0, True)
            return carry

        lax.fori_loop(1, half, both, 0)
        wait_across()
        make_left(points.at[across])
        make_block(0, own_aug)
        backward(half - 1, across, 0, False)
        wait_dir(across)
        forward(across, 0, False)
        low = dirs[partner].astype(jnp.float32)
        acc[3] = direction_out[...] * acc[1] + low * acc[2]

    direction_new = direction_out[...]
    own_terms = direction_new * (acc[0] + ridge * direction_new) + 2.0 * acc[3]
    curv_buf[me] = to_row(jnp.sum(own_terms, axis=1, keepdims=True), TILE)
    send_all(lambda to: curv_buf.at[me], curv_buf, curv_sems)

    if keep:
        last = min(half, early)

        def behind(i, carry):
            k = last - i
            backward(k - 1, near(k), 2 * (k - 1), True)
            return carry

        lax.fori_loop(1, last, behind, 0)
        for k in range(early, half):
            forward(near(k), 2 * (k - 1), True)

    side_send = remote(acc.at[2], side_recv, side_sems.at[0], side_sems.at[1], partner)
    side_send.start()

    if keep:
        forward(across, across_slot, False)

    drain(lambda to: rs_send.at[to], rs_recv, rs_sems)
    drain(lambda to: ag.at[me], ag, ag_sems)
    shared.wait_send()
    for copy in own_left:
        copy.wait_send()
    own_side.wait_send()

    def relay_drain(k, carry):
        for h in range(2):
            hop(k, h, points.at[near(k)], near(k), left).wait_send()
        return carry

    lax.fori_loop(1, half, relay_drain, 0)

    def dir_drain(k, carry):
        dir_to(back(k)).wait_send()
        return carry

    lax.fori_loop(1, half, dir_drain, 0)
    dir_to(taker).wait_send()
    dir_to(partner).wait_send()

    side_send.wait_recv()
    image = acc[0] + acc[1] + ridge * direction_new + side_recv[...]
    for k in range(half):
        image_to(k, across).wait_recv()
        image = image + img_recv[k]
    image_out[...] = image

    wait_all(lambda to: curv_buf.at[me], curv_buf, curv_sems)
    alpha_out[...] = inner_out[...] / jnp.sum(curv_buf[...], axis=0)[:, :outs]
    drain(lambda to: curv_buf.at[me], curv_buf, curv_sems)
    side_send.wait_send()
    for k in range(half):
        image_to(k, across).wait_send()


def finish(
    image_ref,
    direction_ref,
    inner_ref,
    alpha_ref,
    solution_ref,
    residual_ref,
    solution_out,
    residual_out,
    direction_out,
    inner_out,
):
    alpha = to_column(alpha_ref[...])
    direction = direction_ref[...]
    solution_out[...] = solution_ref[...] + alpha * direction
    residual_out[...] = residual_ref[...] - alpha * image_ref[...]
    direction_out[...] = direction
    inner_out[...] = inner_ref[...]


def solution(mesh):
    n = mesh.shape["rows"]

    def local(points, landmarks, chol, ridge, solution, residual, direction, rz_prev):
        feat, own = points.shape
        land = landmarks.shape[1]
        outs = residual.shape[0]
        keep = n <= STORED_BLOCKS
        half = n // 4
        piece = outs * land // (TILE * n)
        padded = -(-(piece + 1) // 8) * 8
        f32, bf16 = jnp.float32, jnp.bfloat16
        vmem = pl.BlockSpec(memory_space=pltpu.VMEM)
        wide = jax.ShapeDtypeStruct((outs, own), f32)
        thin = jax.ShapeDtypeStruct((1, outs), f32)
        dma = pltpu.SemaphoreType.DMA
        results = pl.pallas_call(
            functools.partial(kernel, n, keep),
            out_shape=(wide, wide, thin, thin),
            in_specs=[
                vmem,
                vmem,
                pl.BlockSpec(memory_space=pl.ANY),
                vmem,
                vmem,
                vmem,
                vmem,
            ],
            out_specs=(vmem,) * 4,
            scratch_shapes=[
                pltpu.VMEM((land, land), f32),
                pltpu.VMEM((3, land, land), bf16),
                pltpu.VMEM((3, land // GROUP, GROUP, GROUP), bf16),
                pltpu.VMEM((land // TILE, TILE, TILE), f32),
                pltpu.VMEM((n, feat, own), bf16),
                pltpu.VMEM((feat + 16, own), bf16),
                pltpu.VMEM((feat + 16, own), bf16),
                pltpu.VMEM((feat + 16, own), bf16),
                pltpu.VMEM((2, own, land), bf16),
                pltpu.VMEM((2 * half + 1 if keep else 2, own, own), bf16),
                pltpu.VMEM((n, padded, TILE), f32),
                pltpu.VMEM((n, padded, TILE), f32),
                pltpu.VMEM((n, piece, TILE), f32),
                pltpu.VMEM((outs, land), f32),
                pltpu.VMEM((outs, land), f32),
                pltpu.VMEM((n, outs, own), bf16),
                pltpu.VMEM((4, outs, own), f32),
                pltpu.VMEM((outs, own), f32),
                pltpu.VMEM((half, outs, own), f32),
                pltpu.VMEM((half, outs, own), f32),
                pltpu.VMEM((n, 1, TILE), f32),
                dma,
                dma((2, n)),
                dma((2, n)),
                dma((2, n)),
                dma((2, n)),
                dma((2, half)),
                dma((2,)),
                dma((n, 2)),
                dma((half, 2)),
                dma((2,)),
                dma((2,)),
            ],
            compiler_params=pltpu.CompilerParams(
                collective_id=0, has_side_effects=True, vmem_limit_bytes=62 * 1024 * 1024
            ),
            name="cg_step",
        )(points, landmarks, chol, ridge.reshape(1, 1), residual, direction, rz_prev.reshape(1, outs))
        results = pl.pallas_call(
            finish,
            out_shape=(wide, wide, wide, thin),
            in_specs=[vmem] * 6,
            out_specs=(vmem,) * 4,
            name="finish",
        )(*results, solution, residual)
        return (results[0], results[1], results[2], results[3].reshape(outs))

    wide_spec = P(None, ("groups", "rows"))
    in_specs = (
        wide_spec,
        P(None, "groups"),
        P("groups", None),
        P("groups"),
        wide_spec,
        wide_spec,
        wide_spec,
        P("groups"),
    )
    out_specs = (wide_spec, wide_spec, wide_spec, P("groups"))
    return jax.shard_map(local, mesh=mesh, in_specs=in_specs, out_specs=out_specs, check_vma=False)
```

```python
import functools
import math

import jax
import jax.numpy as jnp
from jax import lax
from jax.experimental import pallas as pl
from jax.experimental.pallas import tpu as pltpu
from jax.sharding import PartitionSpec as P

TILE = 128
CHUNK = 256
GROUP = 2 * TILE
STORED_BLOCKS = 16
LIMIT = 62


def dot_nn(left, right):
    return lax.dot_general(
        left, right, (((1,), (0,)), ((), ())), preferred_element_type=jnp.float32
    )


def dot_nt(left, right):
    return lax.dot_general(
        left, right, (((1,), (1,)), ((), ())), preferred_element_type=jnp.float32
    )


def dot_tn(left, right):
    return lax.dot_general(
        left, right, (((0,), (0,)), ((), ())), preferred_element_type=jnp.float32
    )


def halves(values):
    top = values.astype(jnp.bfloat16)
    return top, (values - top.astype(jnp.float32)).astype(jnp.bfloat16)


def dot_square(left, right):
    width = right.shape[1]
    first, second = halves(right)
    upper = jnp.concatenate([first, second], axis=1)
    lower = jnp.concatenate([jnp.zeros_like(first), first], axis=1)
    both = dot_nn(jnp.concatenate(halves(left), axis=1), jnp.concatenate([upper, lower], axis=0))
    return both[:, :width] + both[:, width:]


def store_pair(ref, at, values):
    for term, part in enumerate(halves(values)):
        ref[(term,) + at] = part


def dot_pair(left, parts, dot):
    outs = left.shape[0]
    top, rest = halves(left)
    high = dot(jnp.concatenate([top, rest], axis=0), parts[0])
    return high[:outs] + (high[outs:] + dot(top, parts[1]))


def norm_rows(features, first):
    wide = features.astype(jnp.float32)
    half = -0.5 * jnp.sum(wide * wide, axis=0, keepdims=True)
    top = half.astype(jnp.bfloat16).astype(jnp.float32)
    rest = half - top
    mid = rest.astype(jnp.bfloat16).astype(jnp.float32)
    low = rest - mid
    row = lax.broadcasted_iota(jnp.int32, (16, features.shape[1]), 0)
    at = 0 if first else 3
    ones = 3 - at
    rows = jnp.where((row >= ones) & (row < ones + 3), 1.0, 0.0)
    rows = jnp.where(row == at, top, rows)
    rows = jnp.where(row == at + 1, mid, rows)
    rows = jnp.where(row == at + 2, low, rows)
    return rows.astype(jnp.bfloat16)


def eye_mask(width):
    shape = (8, width)
    return lax.broadcasted_iota(jnp.int32, shape, 0) == lax.broadcasted_iota(jnp.int32, shape, 1)


def to_row(column, width):
    return jnp.sum(jnp.where(eye_mask(width), column, 0.0), axis=0, keepdims=True)


def to_column(row):
    return jnp.sum(jnp.where(eye_mask(row.shape[1]), row, 0.0), axis=1, keepdims=True)


def kernel(
    n,
    keep,
    points_ref,
    landmarks_ref,
    chol_hbm,
    ridge_ref,
    residual_ref,
    direction_ref,
    rz_ref,
    image_hbm,
    direction_hbm,
    inner_hbm,
    alpha_hbm,
    chol,
    chol_parts,
    inverse_parts,
    inverse,
    points,
    own_aug,
    side_aug,
    col_aug,
    cross,
    kernel_store,
    rs_send,
    rs_recv,
    ag,
    proj,
    work,
    dirs,
    acc,
    side_recv,
    img_send,
    img_recv,
    curv_buf,
    chol_sem,
    rs_sems,
    ag_sems,
    dir_sems,
    curv_sems,
    img_sems,
    side_sems,
    point_recv,
    point_fwd,
    own_sems,
    share_sems,
    image_out,
    direction_out,
    inner_out,
    alpha_out,
    out_sems,
    square_buf,
    square_all,
    square_sems,
    all_sems,
):
    me = lax.axis_index("rows")
    feat, local = points_ref.shape
    land = landmarks_ref.shape[1]
    outs = residual_ref.shape[0]
    chips = n // 2
    half = chips // 2
    core = me % 2
    chip = me // 2
    odd = chip % 2
    pos = (1 - odd) * (chip // 2) + odd * (chips - (chip + 1) // 2)
    scale = math.log2(math.e) / feat

    def row_of(position, lane):
        position = (position + chips) % chips
        upper = position // half
        at = (1 - upper) * (2 * position) + upper * (2 * chips - 1 - 2 * position)
        return at * 2 + (core + lane) % 2

    def remote(src, dst, send, recv, to):
        return pltpu.make_async_remote_copy(
            src_ref=src,
            dst_ref=dst,
            send_sem=send,
            recv_sem=recv,
            device_id={"rows": to},
            device_id_type=pl.DeviceIdType.MESH,
        )

    def others(body):
        lax.fori_loop(1, n, lambda k, carry: (body((me + k) % n), carry)[1], 0)

    def send_all(src_of, buf, sems):
        others(lambda to: remote(src_of(to), buf.at[me], sems.at[0, to], sems.at[1, me], to).start())

    def wait_all(src_of, buf, sems):
        others(lambda to: remote(src_of(to), buf.at[to], sems.at[0, to], sems.at[1, to], to).wait_recv())

    def drain(src_of, buf, sems):
        others(lambda to: remote(src_of(to), buf.at[me], sems.at[0, to], sems.at[1, me], to).wait_send())

    chol_copy = pltpu.make_async_copy(chol_hbm, chol, chol_sem)
    chol_copy.start()

    barrier = pltpu.get_barrier_semaphore()
    others(lambda to: pl.semaphore_signal(
        barrier, inc=1, device_id={"rows": to}, device_id_type=pl.DeviceIdType.MESH))

    upper = pos // half
    partner = row_of(pos, 1)
    left = row_of(pos - 1, 0)
    left_last = row_of(pos - 1, ((pos - 1 + chips) % chips) // half)
    across = row_of(pos + half, upper)
    taker = row_of(pos + half, 1 - upper)

    def near(k):
        return row_of(pos + k, 0)

    def back(k):
        return row_of(pos - k, 0)

    def hop(k, h, src, owner, to):
        part = pl.ds(h * (feat // 2), feat // 2)
        return remote(src.at[part], points.at[owner, part], point_fwd.at[k, h], point_recv.at[owner, h], to)

    own_left = [hop(0, h, points_ref, me, left if half > 1 else left_last) for h in range(2)]
    own_side = remote(points_ref, points.at[me], own_sems.at[0], own_sems.at[1], partner)

    own_aug[0:feat, :] = points_ref[...]
    own_aug[feat:, :] = norm_rows(points_ref[...], True)
    col_aug[0:feat, :] = landmarks_ref[...]
    col_aug[feat:, :] = norm_rows(landmarks_ref[...], False)

    def entries(left_aug, at, right_aug):
        return jnp.exp2(dot_tn(left_aug[:, pl.ds(at, CHUNK)], right_aug[...]) * scale)

    proj[...] = jnp.zeros_like(proj)

    def project(i, carry):
        at = pl.multiple_of(i * CHUNK, CHUNK)
        values = entries(own_aug, at, col_aug)
        top = values.astype(jnp.bfloat16)
        cross[0, pl.ds(at, CHUNK), :] = top
        cross[1, pl.ds(at, CHUNK), :] = (values - top.astype(jnp.float32)).astype(jnp.bfloat16)
        parts = [cross[term, pl.ds(at, CHUNK), :] for term in range(2)]
        proj[...] += dot_pair(residual_ref[:, pl.ds(at, CHUNK)], parts, dot_nn)
        return carry

    lax.fori_loop(0, local // CHUNK, project, 0)
    own_square = to_row(jnp.sum(residual_ref[...] * residual_ref[...], axis=1, keepdims=True), TILE)

    pl.semaphore_wait(barrier, n - 1)

    tiles = land // TILE
    groups = land // GROUP

    base = (n - tiles) // 2
    adds = (me >= base) & (me < base + tiles)
    mine = me - base

    def tile_to(q):
        return remote(rs_send.at[q], rs_recv.at[me], rs_sems.at[0, q], rs_sems.at[1, me], base + q)

    def each_tile(body):
        def one(q, carry):
            @pl.when(base + q != me)
            def _():
                body(q)

            return carry

        lax.fori_loop(0, tiles, one, 0)

    for q in range(tiles):
        rs_send[q] = proj[:, q * TILE:(q + 1) * TILE]
    square_buf[me] = own_square
    each_tile(lambda q: tile_to(q).start())

    def square_to(to):
        return remote(square_buf.at[me], square_buf.at[me], square_sems.at[0], square_sems.at[1 + me], to)

    @pl.when(me != base)
    def _():
        square_to(base).start()

    own_side.start()
    for copy in own_left:
        copy.start()

    def make_left(owner_points):
        col_aug[0:feat, :] = owner_points[...]
        col_aug[feat:, :] = norm_rows(owner_points[...], False)

    def make_block(slot, right_aug):
        for at in range(0, local, CHUNK):
            kernel_store[slot, at:at + CHUNK, :] = entries(col_aug, at, right_aug).astype(jnp.bfloat16)

    chol_copy.wait()

    row = lax.broadcasted_iota(jnp.int32, (TILE, TILE), 0)
    col = lax.broadcasted_iota(jnp.int32, (TILE, TILE), 1)

    share = tiles // 2
    first = core * share

    def own_block(b):
        at = pl.multiple_of((first + b) * TILE, TILE)
        return chol[pl.ds(at, TILE), pl.ds(at, TILE)]

    inverted = [jnp.where(row == col, 1.0 / own_block(b), 0.0) for b in range(share)]
    size = 1
    while size < TILE:
        below = (row // size == col // size + 1) & (row // (2 * size) == col // (2 * size))
        for b in range(share):
            off = jnp.where(below, own_block(b), 0.0)
            if size == 1:
                on_row = jnp.sum(inverted[b], axis=1, keepdims=True)
                on_col = jnp.sum(inverted[b], axis=0, keepdims=True)
                change = on_row * off * on_col
            else:
                change = dot_square(dot_square(inverted[b], off), inverted[b])
            inverted[b] = inverted[b] - change
        size *= 2
    for b in range(share):
        inverse[first + b] = inverted[b]

    shares = inverse.at[pl.ds(first, share)]
    shared = remote(shares, shares, share_sems.at[0], share_sems.at[1], partner)
    shared.start()

    def pass_on(k, h):
        owner = near(k)
        to = left_last if k == half - 1 else left
        hop(k, h, points.at[owner], owner, left).wait_recv()
        hop(k, h, points.at[owner], owner, to).start()

    def pass_on_any(k):
        owner = near(k)
        for h in range(2):
            hop(k, h, points.at[owner], owner, left).wait_recv()

        @pl.when(k < half - 1)
        def _():
            for h in range(2):
                hop(k, h, points.at[owner], owner, left).start()

        @pl.when(k == half - 1)
        def _():
            for h in range(2):
                hop(k, h, points.at[owner], owner, left_last).start()

    own_slot, side_slot, across_slot = 2 * half - 1, 2 * half, 2 * half - 2

    remote(points_ref, points.at[partner], own_sems.at[0], own_sems.at[1], partner).wait_recv()
    side_aug[0:feat, :] = points[partner]
    side_aug[feat:, :] = norm_rows(points[partner], True)
    def total_to(to):
        return remote(ag.at[mine], ag.at[mine], ag_sems.at[0, to], ag_sems.at[1, mine], to)

    @pl.when(adds)
    def _():
        rs_recv[me] = rs_send[mine]
        others(lambda src: remote(
            rs_send.at[0], rs_recv.at[src], rs_sems.at[0, 0], rs_sems.at[1, src], src).wait_recv())
        ag[mine] = jnp.sum(rs_recv[...], axis=0)
        others(lambda to: total_to(to).start())

    def all_square_to(to):
        return remote(square_all, square_all, all_sems.at[0, to], all_sems.at[1, 0], to)

    @pl.when(me == base)
    def _():
        others(lambda src: remote(
            square_buf.at[src], square_buf.at[src], square_sems.at[0], square_sems.at[1 + src], src).wait_recv())
        square_all[...] = jnp.sum(square_buf[...], axis=0)
        others(lambda to: all_square_to(to).start())

    if half > 1:
        pass_on(1, 0)
    if keep:
        make_left(points_ref)
        make_block(own_slot, own_aug)

    other = inverse.at[pl.ds(share - first, share)]
    remote(other, other, share_sems.at[0], share_sems.at[1], partner).wait_recv()
    for b in range(groups):
        upper_block, lower_block = inverse[2 * b], inverse[2 * b + 1]
        at, end = b * GROUP, (b + 1) * GROUP
        off = chol[at + TILE:end, at:at + TILE]
        change = dot_square(dot_square(lower_block, off), upper_block)
        zero = jnp.zeros_like(upper_block)
        whole = jnp.concatenate(
            [jnp.concatenate([upper_block, zero], axis=1), jnp.concatenate([-change, lower_block], axis=1)], axis=0
        )
        store_pair(inverse_parts, (b,), whole)
        if b > 0:
            store_pair(chol_parts, (slice(at, end), slice(0, at)), chol[at:end, :at])

    def make_pair(k, slot):
        make_left(points.at[near(k)])
        make_block(slot, own_aug)
        make_block(slot + 1, side_aug)

    if half > 1:
        pass_on(1, 1)
    if keep:
        make_left(points.at[partner])
        make_block(side_slot, own_aug)
        if half > 1:
            make_pair(1, 0)
    if half > 2:
        pass_on(2, 0)
    each_tile(lambda q: remote(ag.at[q], ag.at[q], ag_sems.at[0, me], ag_sems.at[1, q], base + q).wait_recv())
    for q in range(tiles):
        work[:, q * TILE:(q + 1) * TILE] = ag[q]
    pieces = [work[:, b * GROUP:(b + 1) * GROUP] for b in range(groups)]

    def block_parts(i, j):
        rows, cols = slice(i * GROUP, (i + 1) * GROUP), slice(j * GROUP, (j + 1) * GROUP)
        return [chol_parts[term, rows, cols] for term in range(2)]

    def inverse_of(b):
        return [inverse_parts[term, b] for term in range(2)]

    for b in range(groups):
        pieces[b] = dot_pair(pieces[b], inverse_of(b), dot_nt)
        for i in range(b + 1, groups):
            pieces[i] = pieces[i] - dot_pair(pieces[b], block_parts(i, b), dot_nt)
    halfway = jnp.concatenate(pieces, axis=1)
    if half > 2:
        pass_on(2, 1)
    for b in reversed(range(groups)):
        pieces[b] = dot_pair(pieces[b], inverse_of(b), dot_nn)
        for j in reversed(range(b)):
            pieces[j] = pieces[j] - dot_pair(pieces[b], block_parts(b, j), dot_nn)
    coeffs = jnp.concatenate(pieces, axis=1)

    ridge = ridge_ref[...]
    @pl.when(me != base)
    def _():
        all_square_to(base).wait_recv()

    square = to_column(square_all[...])
    inner = (square - jnp.sum(halfway * halfway, axis=1, keepdims=True)) / ridge
    inner_out[...] = to_row(inner, TILE)[:, :outs]
    residual = residual_ref[...]
    precond = (residual - dot_pair(coeffs, [cross.at[term][...] for term in range(2)], dot_nt)) / ridge
    direction_new = precond + (inner / to_column(rz_ref[...])) * direction_ref[...]
    direction_out[...] = direction_new
    dirs[me] = direction_new.astype(jnp.bfloat16)

    def copy_out(at, src, dst):
        return pltpu.make_async_copy(src, dst, out_sems.at[at])

    direction_copy = copy_out(0, direction_out, direction_hbm)
    inner_copy = copy_out(1, inner_out, inner_hbm)
    image_copy = copy_out(2, image_out, image_hbm)
    alpha_copy = copy_out(3, alpha_out, alpha_hbm)
    direction_copy.start()
    inner_copy.start()

    def dir_to(to):
        return remote(dirs.at[me], dirs.at[to], dir_sems.at[0, to], dir_sems.at[1, me], to)

    def send_dir(to):
        remote(dirs.at[me], dirs.at[me], dir_sems.at[0, to], dir_sems.at[1, me], to).start()

    def wait_dir(src):
        remote(dirs.at[me], dirs.at[src], dir_sems.at[0, src], dir_sems.at[1, src], src).wait_recv()

    send_dir(taker)
    lax.fori_loop(1, half, lambda k, carry: (send_dir(back(half - k)), carry)[1], 0)
    send_dir(partner)
    if keep and half > 3:
        pass_on(3, 0)

    def wait_across():
        for h in range(2):
            hop(0, h, points.at[across], across, left).wait_recv()

    acc[...] = jnp.zeros_like(acc)

    def forward(owner, slot, side):
        acc[1] += dot_nn(dirs[owner], kernel_store[slot])
        if side:
            acc[2] += dot_nn(dirs[owner], kernel_store[slot + 1])

    def image_to(k, owner):
        return remote(img_send.at[k], img_recv.at[k], img_sems.at[0, k], img_sems.at[1, k], owner)

    def backward(k, owner, slot, side):
        total = dot_nt(dirs[me], kernel_store[slot])
        if side:
            total = total + dot_nt(dirs[partner], kernel_store[slot + 1])
        img_send[k] = total
        image_to(k, owner).start()
        return total

    def at_own(slot):
        acc[0] += dot_nn(dirs[me], kernel_store[slot])

    def at_side(slot):
        acc[0] += dot_nn(dirs[partner], kernel_store[slot])

    early = 3

    def terms_behind(total, owner):
        acc[3] += total * dirs[owner].astype(jnp.float32)

    if keep:
        for k in range(2, half):
            if k > 3:
                pass_on(k, 0)
                pass_on(k, 1)
            make_pair(k, 2 * (k - 1))
            if k == 2 and half > 3:
                pass_on(3, 1)
            if k == 2:
                wait_dir(partner)
            if k >= early:
                sent = backward(k - 1, near(k), 2 * (k - 1), True)
                wait_dir(near(k))
                terms_behind(sent, near(k))
        if half < 3:
            wait_dir(partner)
        at_own(own_slot)
        at_side(side_slot)

        def ahead(k, carry):
            wait_dir(near(k))
            forward(near(k), 2 * (k - 1), True)
            return carry

        lax.fori_loop(1, min(half, early), ahead, 0)
        low = dirs[partner].astype(jnp.float32)
        acc[3] += direction_out[...] * acc[1] + low * acc[2]
        wait_across()
        make_left(points.at[across])
        make_block(across_slot, own_aug)
        sent = backward(half - 1, across, across_slot, False)
        wait_dir(across)
        terms_behind(sent, across)
    else:
        make_left(points_ref)
        make_block(0, own_aug)
        at_own(0)
        make_left(points.at[partner])
        make_block(0, own_aug)
        wait_dir(partner)
        at_side(0)

        def both(k, carry):
            @pl.when(k > 2)
            def _():
                pass_on_any(k)

            make_pair(k, 0)
            backward(k - 1, near(k), 0, True)
            wait_dir(near(k))
            forward(near(k), 0, True)
            return carry

        lax.fori_loop(1, half, both, 0)
        wait_across()
        make_left(points.at[across])
        make_block(0, own_aug)
        backward(half - 1, across, 0, False)
        wait_dir(across)
        forward(across, 0, False)
        low = dirs[partner].astype(jnp.float32)
        acc[3] = direction_out[...] * acc[1] + low * acc[2]

    direction_new = direction_out[...]
    own_terms = direction_new * (acc[0] + ridge * direction_new) + 2.0 * acc[3]
    curv_buf[me] = to_row(jnp.sum(own_terms, axis=1, keepdims=True), TILE)
    send_all(lambda to: curv_buf.at[me], curv_buf, curv_sems)

    if keep:
        last = min(half, early)

        def behind(i, carry):
            k = last - i
            backward(k - 1, near(k), 2 * (k - 1), True)
            return carry

        lax.fori_loop(1, last, behind, 0)
        for k in range(early, half):
            forward(near(k), 2 * (k - 1), True)

    side_send = remote(acc.at[2], side_recv, side_sems.at[0], side_sems.at[1], partner)
    side_send.start()

    if keep:
        forward(across, across_slot, False)

    each_tile(lambda q: tile_to(q).wait_send())

    @pl.when(me != base)
    def _():
        square_to(base).wait_send()

    @pl.when(me == base)
    def _():
        others(lambda to: all_square_to(to).wait_send())

    @pl.when(adds)
    def _():
        others(lambda to: total_to(to).wait_send())

    shared.wait_send()
    for copy in own_left:
        copy.wait_send()
    own_side.wait_send()

    def relay_drain(k, carry):
        for h in range(2):
            hop(k, h, points.at[near(k)], near(k), left).wait_send()
        return carry

    lax.fori_loop(1, half, relay_drain, 0)

    def dir_drain(k, carry):
        dir_to(back(k)).wait_send()
        return carry

    lax.fori_loop(1, half, dir_drain, 0)
    dir_to(taker).wait_send()
    dir_to(partner).wait_send()

    side_send.wait_recv()
    image = acc[0] + acc[1] + ridge * direction_new + side_recv[...]
    for k in range(half):
        image_to(k, across).wait_recv()
        image = image + img_recv[k]
    image_out[...] = image
    image_copy.start()

    wait_all(lambda to: curv_buf.at[me], curv_buf, curv_sems)
    alpha_out[...] = inner_out[...] / jnp.sum(curv_buf[...], axis=0)[:, :outs]
    alpha_copy.start()
    drain(lambda to: curv_buf.at[me], curv_buf, curv_sems)
    side_send.wait_send()
    for k in range(half):
        image_to(k, across).wait_send()
    direction_copy.wait()
    inner_copy.wait()
    image_copy.wait()
    alpha_copy.wait()


def finish(
    image_ref,
    direction_ref,
    inner_ref,
    alpha_ref,
    solution_ref,
    residual_ref,
    solution_out,
    residual_out,
    direction_out,
    inner_out,
):
    alpha = to_column(alpha_ref[...])
    direction = direction_ref[...]
    solution_out[...] = solution_ref[...] + alpha * direction
    residual_out[...] = residual_ref[...] - alpha * image_ref[...]
    direction_out[...] = direction
    inner_out[...] = inner_ref[...]


def solution(mesh):
    n = mesh.shape["rows"]

    def local(points, landmarks, chol, ridge, solution, residual, direction, rz_prev):
        feat, own = points.shape
        land = landmarks.shape[1]
        outs = residual.shape[0]
        keep = n <= STORED_BLOCKS
        half = n // 4
        tiles = land // TILE
        f32, bf16 = jnp.float32, jnp.bfloat16
        vmem = pl.BlockSpec(memory_space=pltpu.VMEM)
        wide = jax.ShapeDtypeStruct((outs, own), f32)
        thin = jax.ShapeDtypeStruct((1, outs), f32)
        dma = pltpu.SemaphoreType.DMA
        anywhere = pl.BlockSpec(memory_space=pl.ANY)
        results = pl.pallas_call(
            functools.partial(kernel, n, keep),
            out_shape=(wide, wide, thin, thin),
            in_specs=[
                vmem,
                vmem,
                pl.BlockSpec(memory_space=pl.ANY),
                vmem,
                vmem,
                vmem,
                vmem,
            ],
            out_specs=(anywhere,) * 4,
            scratch_shapes=[
                pltpu.VMEM((land, land), f32),
                pltpu.VMEM((2, land, land), bf16),
                pltpu.VMEM((2, land // GROUP, GROUP, GROUP), bf16),
                pltpu.VMEM((tiles, TILE, TILE), f32),
                pltpu.VMEM((n, feat, own), bf16),
                pltpu.VMEM((feat + 16, own), bf16),
                pltpu.VMEM((feat + 16, own), bf16),
                pltpu.VMEM((feat + 16, own), bf16),
                pltpu.VMEM((2, own, land), bf16),
                pltpu.VMEM((2 * half + 1 if keep else 2, own, own), bf16),
                pltpu.VMEM((tiles, outs, TILE), f32),
                pltpu.VMEM((n, outs, TILE), f32),
                pltpu.VMEM((tiles, outs, TILE), f32),
                pltpu.VMEM((outs, land), f32),
                pltpu.VMEM((outs, land), f32),
                pltpu.VMEM((n, outs, own), bf16),
                pltpu.VMEM((4, outs, own), f32),
                pltpu.VMEM((outs, own), f32),
                pltpu.VMEM((half, outs, own), f32),
                pltpu.VMEM((half, outs, own), f32),
                pltpu.VMEM((n, 1, TILE), f32),
                dma,
                dma((2, n)),
                dma((2, n)),
                dma((2, n)),
                dma((2, n)),
                dma((2, half)),
                dma((2,)),
                dma((n, 2)),
                dma((half, 2)),
                dma((2,)),
                dma((2,)),
                pltpu.VMEM((outs, own), f32),
                pltpu.VMEM((outs, own), f32),
                pltpu.VMEM((1, outs), f32),
                pltpu.VMEM((1, outs), f32),
                dma((4,)),
                pltpu.VMEM((n, 1, TILE), f32),
                pltpu.VMEM((1, TILE), f32),
                dma((1 + n,)),
                dma((2, n)),
            ],
            compiler_params=pltpu.CompilerParams(
                collective_id=0, has_side_effects=True, vmem_limit_bytes=LIMIT * 1024 * 1024
            ),
            name="cg_step",
        )(points, landmarks, chol, ridge.reshape(1, 1), residual, direction, rz_prev.reshape(1, outs))
        results = pl.pallas_call(
            finish,
            out_shape=(wide, wide, wide, thin),
            in_specs=[vmem] * 6,
            out_specs=(vmem,) * 4,
            name="finish",
        )(*results, solution, residual)
        return (results[0], results[1], results[2], results[3].reshape(outs))

    wide_spec = P(None, ("groups", "rows"))
    in_specs = (
        wide_spec,
        P(None, "groups"),
        P("groups", None),
        P("groups"),
        wide_spec,
        wide_spec,
        wide_spec,
        P("groups"),
    )
    out_specs = (wide_spec, wide_spec, wide_spec, P("groups"))
    return jax.shard_map(local, mesh=mesh, in_specs=in_specs, out_specs=out_specs, check_vma=False)
```

```python
import functools
import math

import jax
import jax.numpy as jnp
from jax import lax
from jax.experimental import pallas as pl
from jax.experimental.pallas import tpu as pltpu
from jax.sharding import PartitionSpec as P

TILE = 128
CHUNK = 256
GROUP = 2 * TILE
STORED_BLOCKS = 16
LIMIT = 62


def dot_nn(left, right):
    return lax.dot_general(
        left, right, (((1,), (0,)), ((), ())), preferred_element_type=jnp.float32
    )


def dot_nt(left, right):
    return lax.dot_general(
        left, right, (((1,), (1,)), ((), ())), preferred_element_type=jnp.float32
    )


def dot_tn(left, right):
    return lax.dot_general(
        left, right, (((0,), (0,)), ((), ())), preferred_element_type=jnp.float32
    )


def halves(values):
    top = values.astype(jnp.bfloat16)
    return top, (values - top.astype(jnp.float32)).astype(jnp.bfloat16)


def dot_square(left, right):
    width = right.shape[1]
    first, second = halves(right)
    upper = jnp.concatenate([first, second], axis=1)
    lower = jnp.concatenate([jnp.zeros_like(first), first], axis=1)
    both = dot_nn(jnp.concatenate(halves(left), axis=1), jnp.concatenate([upper, lower], axis=0))
    return both[:, :width] + both[:, width:]


def store_pair(ref, at, values):
    for term, part in enumerate(halves(values)):
        ref[(term,) + at] = part


def dot_pair(left, parts, dot):
    outs = left.shape[0]
    top, rest = halves(left)
    high = dot(jnp.concatenate([top, rest], axis=0), parts[0])
    return high[:outs] + (high[outs:] + dot(top, parts[1]))


def norm_rows(features, first):
    wide = features.astype(jnp.float32)
    half = -0.5 * jnp.sum(wide * wide, axis=0, keepdims=True)
    top = half.astype(jnp.bfloat16).astype(jnp.float32)
    rest = half - top
    mid = rest.astype(jnp.bfloat16).astype(jnp.float32)
    low = rest - mid
    row = lax.broadcasted_iota(jnp.int32, (16, features.shape[1]), 0)
    at = 0 if first else 3
    ones = 3 - at
    rows = jnp.where((row >= ones) & (row < ones + 3), 1.0, 0.0)
    rows = jnp.where(row == at, top, rows)
    rows = jnp.where(row == at + 1, mid, rows)
    rows = jnp.where(row == at + 2, low, rows)
    return rows.astype(jnp.bfloat16)


def eye_mask(width):
    shape = (8, width)
    return lax.broadcasted_iota(jnp.int32, shape, 0) == lax.broadcasted_iota(jnp.int32, shape, 1)


def to_row(column, width):
    return jnp.sum(jnp.where(eye_mask(width), column, 0.0), axis=0, keepdims=True)


def to_column(row):
    return jnp.sum(jnp.where(eye_mask(row.shape[1]), row, 0.0), axis=1, keepdims=True)


def kernel(
    n,
    keep,
    points_ref,
    landmarks_ref,
    chol_hbm,
    ridge_ref,
    residual_ref,
    direction_ref,
    rz_ref,
    image_hbm,
    direction_hbm,
    inner_hbm,
    alpha_hbm,
    chol,
    chol_parts,
    inverse_parts,
    inverse,
    points,
    own_aug,
    side_aug,
    col_aug,
    cross,
    kernel_store,
    rs_send,
    rs_recv,
    ag,
    proj,
    work,
    dirs,
    acc,
    side_recv,
    img_send,
    img_recv,
    curv_buf,
    chol_sem,
    rs_sems,
    ag_sems,
    dir_sems,
    curv_sems,
    img_sems,
    side_sems,
    point_recv,
    point_fwd,
    own_sems,
    share_sems,
    image_out,
    direction_out,
    inner_out,
    alpha_out,
    out_sems,
    square_buf,
    square_all,
    square_sems,
    all_sems,
):
    me = lax.axis_index("rows")
    feat, local = points_ref.shape
    land = landmarks_ref.shape[1]
    outs = residual_ref.shape[0]
    chips = n // 2
    half = chips // 2
    core = me % 2
    chip = me // 2
    odd = chip % 2
    pos = (1 - odd) * (chip // 2) + odd * (chips - (chip + 1) // 2)
    scale = math.log2(math.e) / feat

    def row_of(position, lane):
        position = (position + chips) % chips
        upper = position // half
        at = (1 - upper) * (2 * position) + upper * (2 * chips - 1 - 2 * position)
        return at * 2 + (core + lane) % 2

    def remote(src, dst, send, recv, to):
        return pltpu.make_async_remote_copy(
            src_ref=src,
            dst_ref=dst,
            send_sem=send,
            recv_sem=recv,
            device_id={"rows": to},
            device_id_type=pl.DeviceIdType.MESH,
        )

    def others(body):
        lax.fori_loop(1, n, lambda k, carry: (body((me + k) % n), carry)[1], 0)

    def send_all(src_of, buf, sems):
        others(lambda to: remote(src_of(to), buf.at[me], sems.at[0, to], sems.at[1, me], to).start())

    def wait_all(src_of, buf, sems):
        others(lambda to: remote(src_of(to), buf.at[to], sems.at[0, to], sems.at[1, to], to).wait_recv())

    def drain(src_of, buf, sems):
        others(lambda to: remote(src_of(to), buf.at[me], sems.at[0, to], sems.at[1, me], to).wait_send())

    chol_copy = pltpu.make_async_copy(chol_hbm, chol, chol_sem)
    chol_copy.start()

    upper = pos // half
    partner = row_of(pos, 1)
    left = row_of(pos - 1, 0)
    left_last = row_of(pos - 1, ((pos - 1 + chips) % chips) // half)
    across = row_of(pos + half, upper)
    taker = row_of(pos + half, 1 - upper)

    tiles = land // TILE
    base = (n - tiles) // 2
    adds = (me >= base) & (me < base + tiles)
    mine = me - base

    barrier = pltpu.get_barrier_semaphore()

    def greet(to):
        pl.semaphore_signal(barrier, inc=1, device_id={"rows": to}, device_id_type=pl.DeviceIdType.MESH)

    greet(partner)
    greet(row_of(pos + 1, 0))
    greet(row_of(pos + 1, 1))

    @pl.when(adds)
    def _():
        others(greet)

    def near(k):
        return row_of(pos + k, 0)

    def back(k):
        return row_of(pos - k, 0)

    def hop(k, h, src, owner, to):
        part = pl.ds(h * (feat // 2), feat // 2)
        return remote(src.at[part], points.at[owner, part], point_fwd.at[k, h], point_recv.at[owner, h], to)

    own_left = [hop(0, h, points_ref, me, left if half > 1 else left_last) for h in range(2)]
    own_side = remote(points_ref, points.at[me], own_sems.at[0], own_sems.at[1], partner)

    own_aug[0:feat, :] = points_ref[...]
    own_aug[feat:, :] = norm_rows(points_ref[...], True)
    col_aug[0:feat, :] = landmarks_ref[...]
    col_aug[feat:, :] = norm_rows(landmarks_ref[...], False)

    def entries(left_aug, at, right_aug):
        return jnp.exp2(dot_tn(left_aug[:, pl.ds(at, CHUNK)], right_aug[...]) * scale)

    proj[...] = jnp.zeros_like(proj)

    for at in range(0, local, CHUNK):
        values = entries(own_aug, at, col_aug)
        top = values.astype(jnp.bfloat16)
        cross[0, pl.ds(at, CHUNK), :] = top
        cross[1, pl.ds(at, CHUNK), :] = (values - top.astype(jnp.float32)).astype(jnp.bfloat16)
        parts = [cross[term, pl.ds(at, CHUNK), :] for term in range(2)]
        proj[...] += dot_pair(residual_ref[:, pl.ds(at, CHUNK)], parts, dot_nn)
    own_square = to_row(jnp.sum(residual_ref[...] * residual_ref[...], axis=1, keepdims=True), TILE)

    pl.semaphore_wait(barrier, tiles + 3 - jnp.where(adds, 1, 0))

    groups = land // GROUP

    def tile_to(q):
        return remote(rs_send.at[q], rs_recv.at[me], rs_sems.at[0, q], rs_sems.at[1, me], base + q)

    def each_tile(body):
        def one(q, carry):
            @pl.when(base + q != me)
            def _():
                body(q)

            return carry

        lax.fori_loop(0, tiles, one, 0)

    for q in range(tiles):
        rs_send[q] = proj[:, q * TILE:(q + 1) * TILE]
    square_buf[me] = own_square
    each_tile(lambda q: tile_to(q).start())

    def square_to(to):
        return remote(square_buf.at[me], square_buf.at[me], square_sems.at[0], square_sems.at[1 + me], to)

    @pl.when(me != base)
    def _():
        square_to(base).start()

    own_side.start()
    for copy in own_left:
        copy.start()

    def make_left(owner_points):
        col_aug[0:feat, :] = owner_points[...]
        col_aug[feat:, :] = norm_rows(owner_points[...], False)

    def make_block(slot, right_aug):
        for at in range(0, local, CHUNK):
            kernel_store[slot, at:at + CHUNK, :] = entries(col_aug, at, right_aug).astype(jnp.bfloat16)

    chol_copy.wait()

    row = lax.broadcasted_iota(jnp.int32, (TILE, TILE), 0)
    col = lax.broadcasted_iota(jnp.int32, (TILE, TILE), 1)

    share = tiles // 2
    first = core * share

    def own_block(b):
        at = pl.multiple_of((first + b) * TILE, TILE)
        return chol[pl.ds(at, TILE), pl.ds(at, TILE)]

    inverted = [jnp.where(row == col, 1.0 / own_block(b), 0.0) for b in range(share)]
    size = 1
    while size < TILE:
        below = (row // size == col // size + 1) & (row // (2 * size) == col // (2 * size))
        for b in range(share):
            off = jnp.where(below, own_block(b), 0.0)
            if size == 1:
                on_row = jnp.sum(inverted[b], axis=1, keepdims=True)
                on_col = jnp.sum(inverted[b], axis=0, keepdims=True)
                change = on_row * off * on_col
            else:
                change = dot_square(dot_square(inverted[b], off), inverted[b])
            inverted[b] = inverted[b] - change
        size *= 2
    for b in range(share):
        inverse[first + b] = inverted[b]

    shares = inverse.at[pl.ds(first, share)]
    shared = remote(shares, shares, share_sems.at[0], share_sems.at[1], partner)
    shared.start()

    def pass_on(k, h):
        owner = near(k)
        to = left_last if k == half - 1 else left
        hop(k, h, points.at[owner], owner, left).wait_recv()
        hop(k, h, points.at[owner], owner, to).start()

    def pass_on_any(k):
        owner = near(k)
        for h in range(2):
            hop(k, h, points.at[owner], owner, left).wait_recv()

        @pl.when(k < half - 1)
        def _():
            for h in range(2):
                hop(k, h, points.at[owner], owner, left).start()

        @pl.when(k == half - 1)
        def _():
            for h in range(2):
                hop(k, h, points.at[owner], owner, left_last).start()

    own_slot, side_slot, across_slot = 2 * half - 1, 2 * half, 2 * half - 2

    remote(points_ref, points.at[partner], own_sems.at[0], own_sems.at[1], partner).wait_recv()
    side_aug[0:feat, :] = points[partner]
    side_aug[feat:, :] = norm_rows(points[partner], True)
    if keep:
        make_left(points_ref)
        make_block(own_slot, own_aug)
        make_left(points.at[partner])
        make_block(side_slot, own_aug)
    if half > 1:
        @pl.when(jnp.logical_not(adds))
        def _():
            pass_on(1, 0)

    other = inverse.at[pl.ds(share - first, share)]
    remote(other, other, share_sems.at[0], share_sems.at[1], partner).wait_recv()
    for b in range(groups):
        upper_block, lower_block = inverse[2 * b], inverse[2 * b + 1]
        at, end = b * GROUP, (b + 1) * GROUP
        off = chol[at + TILE:end, at:at + TILE]
        change = dot_square(dot_square(lower_block, off), upper_block)
        zero = jnp.zeros_like(upper_block)
        whole = jnp.concatenate(
            [jnp.concatenate([upper_block, zero], axis=1), jnp.concatenate([-change, lower_block], axis=1)], axis=0
        )
        store_pair(inverse_parts, (b,), whole)
        if b > 0:
            store_pair(chol_parts, (slice(at, end), slice(0, at)), chol[at:end, :at])

    def make_pair(k, slot):
        make_left(points.at[near(k)])
        make_block(slot, own_aug)
        make_block(slot + 1, side_aug)

    def total_to(to):
        return remote(ag.at[mine], ag.at[mine], ag_sems.at[0, to], ag_sems.at[1, mine], to)

    @pl.when(adds)
    def _():
        rs_recv[me] = rs_send[mine]
        others(lambda src: remote(
            rs_send.at[0], rs_recv.at[src], rs_sems.at[0, 0], rs_sems.at[1, src], src).wait_recv())
        ag[mine] = jnp.sum(rs_recv[...], axis=0)
        others(lambda to: total_to(to).start())
        if half > 1:
            pass_on(1, 0)

    def all_square_to(to):
        return remote(square_all, square_all, all_sems.at[0, to], all_sems.at[1, 0], to)

    @pl.when(me == base)
    def _():
        others(lambda src: remote(
            square_buf.at[src], square_buf.at[src], square_sems.at[0], square_sems.at[1 + src], src).wait_recv())
        square_all[...] = jnp.sum(square_buf[...], axis=0)
        others(lambda to: all_square_to(to).start())

    if half > 1:
        pass_on(1, 1)
    if keep and half > 1:
        make_pair(1, 0)
    each_tile(lambda q: remote(ag.at[q], ag.at[q], ag_sems.at[0, me], ag_sems.at[1, q], base + q).wait_recv())
    for q in range(tiles):
        work[:, q * TILE:(q + 1) * TILE] = ag[q]
    pieces = [work[:, b * GROUP:(b + 1) * GROUP] for b in range(groups)]

    def block_parts(i, j):
        rows, cols = slice(i * GROUP, (i + 1) * GROUP), slice(j * GROUP, (j + 1) * GROUP)
        return [chol_parts[term, rows, cols] for term in range(2)]

    def inverse_of(b):
        return [inverse_parts[term, b] for term in range(2)]

    for b in range(groups):
        pieces[b] = dot_pair(pieces[b], inverse_of(b), dot_nt)
        for i in range(b + 1, groups):
            pieces[i] = pieces[i] - dot_pair(pieces[b], block_parts(i, b), dot_nt)
    halfway = jnp.concatenate(pieces, axis=1)
    if half > 2:
        pass_on(2, 0)
    for b in reversed(range(groups)):
        pieces[b] = dot_pair(pieces[b], inverse_of(b), dot_nn)
        for j in reversed(range(b)):
            pieces[j] = pieces[j] - dot_pair(pieces[b], block_parts(b, j), dot_nn)
    coeffs = jnp.concatenate(pieces, axis=1)
    if half > 2:
        pass_on(2, 1)

    ridge = ridge_ref[...]
    @pl.when(me != base)
    def _():
        all_square_to(base).wait_recv()

    square = to_column(square_all[...])
    inner = (square - jnp.sum(halfway * halfway, axis=1, keepdims=True)) / ridge
    inner_out[...] = to_row(inner, TILE)[:, :outs]
    residual = residual_ref[...]
    precond = (residual - dot_pair(coeffs, [cross.at[term][...] for term in range(2)], dot_nt)) / ridge
    direction_new = precond + (inner / to_column(rz_ref[...])) * direction_ref[...]
    direction_out[...] = direction_new
    dirs[me] = direction_new.astype(jnp.bfloat16)

    def copy_out(at, src, dst):
        return pltpu.make_async_copy(src, dst, out_sems.at[at])

    direction_copy = copy_out(0, direction_out, direction_hbm)
    inner_copy = copy_out(1, inner_out, inner_hbm)
    image_copy = copy_out(2, image_out, image_hbm)
    alpha_copy = copy_out(3, alpha_out, alpha_hbm)
    direction_copy.start()
    inner_copy.start()

    def dir_to(to):
        return remote(dirs.at[me], dirs.at[to], dir_sems.at[0, to], dir_sems.at[1, me], to)

    def send_dir(to):
        remote(dirs.at[me], dirs.at[me], dir_sems.at[0, to], dir_sems.at[1, me], to).start()

    def wait_dir(src):
        remote(dirs.at[me], dirs.at[src], dir_sems.at[0, src], dir_sems.at[1, src], src).wait_recv()

    send_dir(taker)
    lax.fori_loop(1, half, lambda k, carry: (send_dir(back(half - k)), carry)[1], 0)
    send_dir(partner)
    def wait_across():
        for h in range(2):
            hop(0, h, points.at[across], across, left).wait_recv()

    acc[...] = jnp.zeros_like(acc)

    def forward(owner, slot, side):
        acc[1] += dot_nn(dirs[owner], kernel_store[slot])
        if side:
            acc[2] += dot_nn(dirs[owner], kernel_store[slot + 1])

    def image_to(k, owner):
        return remote(img_send.at[k], img_recv.at[k], img_sems.at[0, k], img_sems.at[1, k], owner)

    def backward(k, owner, slot, side):
        total = dot_nt(dirs[me], kernel_store[slot])
        if side:
            total = total + dot_nt(dirs[partner], kernel_store[slot + 1])
        img_send[k] = total
        image_to(k, owner).start()
        return total

    def at_own(slot):
        acc[0] += dot_nn(dirs[me], kernel_store[slot])

    def at_side(slot):
        acc[0] += dot_nn(dirs[partner], kernel_store[slot])

    early = 3

    def terms_behind(total, owner):
        acc[3] += total * dirs[owner].astype(jnp.float32)

    if keep:
        if half > 2:
            make_pair(2, 2)
        if half > 3:
            pass_on(3, 0)
        wait_dir(partner)
        at_own(own_slot)
        at_side(side_slot)
        if half > 3:
            pass_on(3, 1)

        def ahead(k, carry):
            wait_dir(near(k))
            forward(near(k), 2 * (k - 1), True)
            return carry

        lax.fori_loop(1, min(half, early), ahead, 0)
        low = dirs[partner].astype(jnp.float32)
        acc[3] = direction_out[...] * acc[1] + low * acc[2]
        for k in range(early, half):
            if k > 3:
                pass_on(k, 0)
                pass_on(k, 1)
            make_pair(k, 2 * (k - 1))
            sent = backward(k - 1, near(k), 2 * (k - 1), True)
            wait_dir(near(k))
            terms_behind(sent, near(k))
        wait_across()
        make_left(points.at[across])
        make_block(across_slot, own_aug)
        sent = backward(half - 1, across, across_slot, False)
        wait_dir(across)
        terms_behind(sent, across)
    else:
        make_left(points_ref)
        make_block(0, own_aug)
        at_own(0)
        make_left(points.at[partner])
        make_block(0, own_aug)
        wait_dir(partner)
        at_side(0)

        def both(k, carry):
            @pl.when(k > 2)
            def _():
                pass_on_any(k)

            make_pair(k, 0)
            backward(k - 1, near(k), 0, True)
            wait_dir(near(k))
            forward(near(k), 0, True)
            return carry

        lax.fori_loop(1, half, both, 0)
        wait_across()
        make_left(points.at[across])
        make_block(0, own_aug)
        backward(half - 1, across, 0, False)
        wait_dir(across)
        forward(across, 0, False)
        low = dirs[partner].astype(jnp.float32)
        acc[3] = direction_out[...] * acc[1] + low * acc[2]

    direction_new = direction_out[...]
    own_terms = direction_new * (acc[0] + ridge * direction_new) + 2.0 * acc[3]
    curv_buf[me] = to_row(jnp.sum(own_terms, axis=1, keepdims=True), TILE)
    send_all(lambda to: curv_buf.at[me], curv_buf, curv_sems)

    if keep:
        last = min(half, early)

        def behind(i, carry):
            k = last - i
            backward(k - 1, near(k), 2 * (k - 1), True)
            return carry

        lax.fori_loop(1, last, behind, 0)
        for k in range(early, half):
            forward(near(k), 2 * (k - 1), True)

    side_send = remote(acc.at[2], side_recv, side_sems.at[0], side_sems.at[1], partner)
    side_send.start()

    if keep:
        forward(across, across_slot, False)

    each_tile(lambda q: tile_to(q).wait_send())

    @pl.when(me != base)
    def _():
        square_to(base).wait_send()

    @pl.when(me == base)
    def _():
        others(lambda to: all_square_to(to).wait_send())

    @pl.when(adds)
    def _():
        others(lambda to: total_to(to).wait_send())

    shared.wait_send()
    for copy in own_left:
        copy.wait_send()
    own_side.wait_send()

    def relay_drain(k, carry):
        for h in range(2):
            hop(k, h, points.at[near(k)], near(k), left).wait_send()
        return carry

    lax.fori_loop(1, half, relay_drain, 0)

    def dir_drain(k, carry):
        dir_to(back(k)).wait_send()
        return carry

    lax.fori_loop(1, half, dir_drain, 0)
    dir_to(taker).wait_send()
    dir_to(partner).wait_send()

    side_send.wait_recv()
    image = acc[0] + acc[1] + ridge * direction_new + side_recv[...]
    for k in range(half):
        image_to(k, across).wait_recv()
        image = image + img_recv[k]
    image_out[...] = image
    image_copy.start()

    wait_all(lambda to: curv_buf.at[me], curv_buf, curv_sems)
    alpha_out[...] = inner_out[...] / jnp.sum(curv_buf[...], axis=0)[:, :outs]
    alpha_copy.start()
    drain(lambda to: curv_buf.at[me], curv_buf, curv_sems)
    side_send.wait_send()
    for k in range(half):
        image_to(k, across).wait_send()
    direction_copy.wait()
    inner_copy.wait()
    image_copy.wait()
    alpha_copy.wait()


def finish(
    image_ref,
    direction_ref,
    inner_ref,
    alpha_ref,
    solution_ref,
    residual_ref,
    solution_out,
    residual_out,
    direction_out,
    inner_out,
):
    alpha = to_column(alpha_ref[...])
    direction = direction_ref[...]
    solution_out[...] = solution_ref[...] + alpha * direction
    residual_out[...] = residual_ref[...] - alpha * image_ref[...]
    direction_out[...] = direction
    inner_out[...] = inner_ref[...]


def solution(mesh):
    n = mesh.shape["rows"]

    def local(points, landmarks, chol, ridge, solution, residual, direction, rz_prev):
        feat, own = points.shape
        land = landmarks.shape[1]
        outs = residual.shape[0]
        keep = n <= STORED_BLOCKS
        half = n // 4
        tiles = land // TILE
        f32, bf16 = jnp.float32, jnp.bfloat16
        vmem = pl.BlockSpec(memory_space=pltpu.VMEM)
        wide = jax.ShapeDtypeStruct((outs, own), f32)
        thin = jax.ShapeDtypeStruct((1, outs), f32)
        dma = pltpu.SemaphoreType.DMA
        anywhere = pl.BlockSpec(memory_space=pl.ANY)
        results = pl.pallas_call(
            functools.partial(kernel, n, keep),
            out_shape=(wide, wide, thin, thin),
            in_specs=[
                vmem,
                vmem,
                pl.BlockSpec(memory_space=pl.ANY),
                vmem,
                vmem,
                vmem,
                vmem,
            ],
            out_specs=(anywhere,) * 4,
            scratch_shapes=[
                pltpu.VMEM((land, land), f32),
                pltpu.VMEM((2, land, land), bf16),
                pltpu.VMEM((2, land // GROUP, GROUP, GROUP), bf16),
                pltpu.VMEM((tiles, TILE, TILE), f32),
                pltpu.VMEM((n, feat, own), bf16),
                pltpu.VMEM((feat + 16, own), bf16),
                pltpu.VMEM((feat + 16, own), bf16),
                pltpu.VMEM((feat + 16, own), bf16),
                pltpu.VMEM((2, own, land), bf16),
                pltpu.VMEM((2 * half + 1 if keep else 2, own, own), bf16),
                pltpu.VMEM((tiles, outs, TILE), f32),
                pltpu.VMEM((n, outs, TILE), f32),
                pltpu.VMEM((tiles, outs, TILE), f32),
                pltpu.VMEM((outs, land), f32),
                pltpu.VMEM((outs, land), f32),
                pltpu.VMEM((n, outs, own), bf16),
                pltpu.VMEM((4, outs, own), f32),
                pltpu.VMEM((outs, own), f32),
                pltpu.VMEM((half, outs, own), f32),
                pltpu.VMEM((half, outs, own), f32),
                pltpu.VMEM((n, 1, TILE), f32),
                dma,
                dma((2, n)),
                dma((2, n)),
                dma((2, n)),
                dma((2, n)),
                dma((2, half)),
                dma((2,)),
                dma((n, 2)),
                dma((half, 2)),
                dma((2,)),
                dma((2,)),
                pltpu.VMEM((outs, own), f32),
                pltpu.VMEM((outs, own), f32),
                pltpu.VMEM((1, outs), f32),
                pltpu.VMEM((1, outs), f32),
                dma((4,)),
                pltpu.VMEM((n, 1, TILE), f32),
                pltpu.VMEM((1, TILE), f32),
                dma((1 + n,)),
                dma((2, n)),
            ],
            compiler_params=pltpu.CompilerParams(
                collective_id=0, has_side_effects=True, vmem_limit_bytes=LIMIT * 1024 * 1024
            ),
            name="cg_step",
        )(points, landmarks, chol, ridge.reshape(1, 1), residual, direction, rz_prev.reshape(1, outs))
        results = pl.pallas_call(
            finish,
            out_shape=(wide, wide, wide, thin),
            in_specs=[vmem] * 6,
            out_specs=(vmem,) * 4,
            name="finish",
        )(*results, solution, residual)
        return (results[0], results[1], results[2], results[3].reshape(outs))

    wide_spec = P(None, ("groups", "rows"))
    in_specs = (
        wide_spec,
        P(None, "groups"),
        P("groups", None),
        P("groups"),
        wide_spec,
        wide_spec,
        wide_spec,
        P("groups"),
    )
    out_specs = (wide_spec, wide_spec, wide_spec, P("groups"))
    return jax.shard_map(local, mesh=mesh, in_specs=in_specs, out_specs=out_specs, check_vma=False)
```

```python
import functools
import math

import jax
import jax.numpy as jnp
from jax import lax
from jax.experimental import pallas as pl
from jax.experimental.pallas import tpu as pltpu
from jax.sharding import PartitionSpec as P

TILE = 128
CHUNK = 256
GROUP = 2 * TILE
STORED_BLOCKS = 16
LIMIT = 62


def dot_nn(left, right):
    return lax.dot_general(
        left, right, (((1,), (0,)), ((), ())), preferred_element_type=jnp.float32
    )


def dot_nt(left, right):
    return lax.dot_general(
        left, right, (((1,), (1,)), ((), ())), preferred_element_type=jnp.float32
    )


def dot_tn(left, right):
    return lax.dot_general(
        left, right, (((0,), (0,)), ((), ())), preferred_element_type=jnp.float32
    )


def halves(values):
    top = values.astype(jnp.bfloat16)
    return top, (values - top.astype(jnp.float32)).astype(jnp.bfloat16)


def dot_square(left, right):
    width = right.shape[1]
    first, second = halves(right)
    upper = jnp.concatenate([first, second], axis=1)
    lower = jnp.concatenate([jnp.zeros_like(first), first], axis=1)
    both = dot_nn(jnp.concatenate(halves(left), axis=1), jnp.concatenate([upper, lower], axis=0))
    return both[:, :width] + both[:, width:]


def store_pair(ref, at, values):
    for term, part in enumerate(halves(values)):
        ref[(term,) + at] = part


def dot_pair(left, parts, dot):
    outs = left.shape[0]
    top, rest = halves(left)
    high = dot(jnp.concatenate([top, rest], axis=0), parts[0])
    return high[:outs] + (high[outs:] + dot(top, parts[1]))


def norm_rows(features, first):
    wide = features.astype(jnp.float32)
    half = -0.5 * jnp.sum(wide * wide, axis=0, keepdims=True)
    top = half.astype(jnp.bfloat16).astype(jnp.float32)
    rest = half - top
    mid = rest.astype(jnp.bfloat16).astype(jnp.float32)
    low = rest - mid
    row = lax.broadcasted_iota(jnp.int32, (16, features.shape[1]), 0)
    at = 0 if first else 3
    ones = 3 - at
    rows = jnp.where((row >= ones) & (row < ones + 3), 1.0, 0.0)
    rows = jnp.where(row == at, top, rows)
    rows = jnp.where(row == at + 1, mid, rows)
    rows = jnp.where(row == at + 2, low, rows)
    return rows.astype(jnp.bfloat16)


def eye_mask(width):
    shape = (8, width)
    return lax.broadcasted_iota(jnp.int32, shape, 0) == lax.broadcasted_iota(jnp.int32, shape, 1)


def to_row(column, width):
    return jnp.sum(jnp.where(eye_mask(width), column, 0.0), axis=0, keepdims=True)


def to_column(row):
    return jnp.sum(jnp.where(eye_mask(row.shape[1]), row, 0.0), axis=1, keepdims=True)


def kernel(
    n,
    keep,
    points_ref,
    landmarks_ref,
    chol_hbm,
    ridge_ref,
    residual_ref,
    direction_ref,
    rz_ref,
    image_hbm,
    direction_hbm,
    inner_hbm,
    alpha_hbm,
    chol,
    chol_parts,
    inverse_parts,
    inverse,
    points,
    own_aug,
    side_aug,
    col_aug,
    cross,
    kernel_store,
    rs_send,
    rs_recv,
    ag,
    proj,
    work,
    dirs,
    acc,
    side_recv,
    img_send,
    img_recv,
    curv_buf,
    chol_sem,
    rs_sems,
    ag_sems,
    dir_sems,
    curv_sems,
    img_sems,
    side_sems,
    point_recv,
    point_fwd,
    own_sems,
    share_sems,
    image_out,
    direction_out,
    inner_out,
    alpha_out,
    out_sems,
    square_buf,
    square_all,
    square_sems,
    all_sems,
):
    me = lax.axis_index("rows")
    feat, local = points_ref.shape
    land = landmarks_ref.shape[1]
    outs = residual_ref.shape[0]
    chips = n // 2
    half = chips // 2
    core = me % 2
    chip = me // 2
    odd = chip % 2
    pos = (1 - odd) * (chip // 2) + odd * (chips - (chip + 1) // 2)
    scale = math.log2(math.e) / feat

    def row_of(position, lane):
        position = (position + chips) % chips
        upper = position // half
        at = (1 - upper) * (2 * position) + upper * (2 * chips - 1 - 2 * position)
        return at * 2 + (core + lane) % 2

    def remote(src, dst, send, recv, to):
        return pltpu.make_async_remote_copy(
            src_ref=src,
            dst_ref=dst,
            send_sem=send,
            recv_sem=recv,
            device_id={"rows": to},
            device_id_type=pl.DeviceIdType.MESH,
        )

    def others(body):
        lax.fori_loop(1, n, lambda k, carry: (body((me + k) % n), carry)[1], 0)

    def send_all(src_of, buf, sems):
        others(lambda to: remote(src_of(to), buf.at[me], sems.at[0, to], sems.at[1, me], to).start())

    def wait_all(src_of, buf, sems):
        others(lambda to: remote(src_of(to), buf.at[to], sems.at[0, to], sems.at[1, to], to).wait_recv())

    def drain(src_of, buf, sems):
        others(lambda to: remote(src_of(to), buf.at[me], sems.at[0, to], sems.at[1, me], to).wait_send())

    chol_copy = pltpu.make_async_copy(chol_hbm, chol, chol_sem)
    chol_copy.start()

    upper = pos // half
    partner = row_of(pos, 1)
    left = row_of(pos - 1, 0)
    left_last = row_of(pos - 1, ((pos - 1 + chips) % chips) // half)
    across = row_of(pos + half, upper)
    taker = row_of(pos + half, 1 - upper)

    tiles = land // TILE
    base = (n - tiles) // 2
    adds = (me >= base) & (me < base + tiles)
    mine = me - base

    barrier = pltpu.get_barrier_semaphore()

    def greet(to):
        pl.semaphore_signal(barrier, inc=1, device_id={"rows": to}, device_id_type=pl.DeviceIdType.MESH)

    greet(partner)
    greet(row_of(pos + 1, 0))
    greet(row_of(pos + 1, 1))

    @pl.when(adds)
    def _():
        others(greet)

    def near(k):
        return row_of(pos + k, 0)

    def back(k):
        return row_of(pos - k, 0)

    def hop(k, h, src, owner, to):
        part = pl.ds(h * (feat // 2), feat // 2)
        return remote(src.at[part], points.at[owner, part], point_fwd.at[k, h], point_recv.at[owner, h], to)

    own_left = [hop(0, h, points_ref, me, left if half > 1 else left_last) for h in range(2)]
    own_side = remote(points_ref, points.at[me], own_sems.at[0], own_sems.at[1], partner)

    own_aug[0:feat, :] = points_ref[...]
    own_aug[feat:, :] = norm_rows(points_ref[...], True)
    col_aug[0:feat, :] = landmarks_ref[...]
    col_aug[feat:, :] = norm_rows(landmarks_ref[...], False)

    def entries(left_aug, at, right_aug):
        return jnp.exp2(dot_tn(left_aug[:, pl.ds(at, CHUNK)], right_aug[...]) * scale)

    proj[...] = jnp.zeros_like(proj)

    for at in range(0, local, CHUNK):
        values = entries(own_aug, at, col_aug)
        top = values.astype(jnp.bfloat16)
        cross[0, pl.ds(at, CHUNK), :] = top
        cross[1, pl.ds(at, CHUNK), :] = (values - top.astype(jnp.float32)).astype(jnp.bfloat16)
        parts = [cross[term, pl.ds(at, CHUNK), :] for term in range(2)]
        proj[...] += dot_pair(residual_ref[:, pl.ds(at, CHUNK)], parts, dot_nn)

    own_square = to_row(jnp.sum(residual_ref[...] * residual_ref[...], axis=1, keepdims=True), TILE)

    pl.semaphore_wait(barrier, tiles + 3 - jnp.where(adds, 1, 0))

    groups = land // GROUP

    def tile_to(q):
        return remote(rs_send.at[q], rs_recv.at[me], rs_sems.at[0, q], rs_sems.at[1, me], base + q)

    def each_tile(body):
        def one(q, carry):
            @pl.when(base + q != me)
            def _():
                body(q)

            return carry

        lax.fori_loop(0, tiles, one, 0)

    for q in range(tiles):
        rs_send[q] = proj[:, q * TILE:(q + 1) * TILE]
    square_buf[me] = own_square
    each_tile(lambda q: tile_to(q).start())

    def square_to(to):
        return remote(square_buf.at[me], square_buf.at[me], square_sems.at[0], square_sems.at[1 + me], to)

    @pl.when(me != base)
    def _():
        square_to(base).start()

    own_side.start()
    for copy in own_left:
        copy.start()

    def make_left(owner_points):
        col_aug[0:feat, :] = owner_points[...]
        col_aug[feat:, :] = norm_rows(owner_points[...], False)

    def make_block(slot, right_aug):
        for at in range(0, local, CHUNK):
            kernel_store[slot, at:at + CHUNK, :] = entries(col_aug, at, right_aug).astype(jnp.bfloat16)

    chol_copy.wait()

    row = lax.broadcasted_iota(jnp.int32, (TILE, TILE), 0)
    col = lax.broadcasted_iota(jnp.int32, (TILE, TILE), 1)

    share = tiles // 2
    first = core * share

    def own_block(b):
        at = pl.multiple_of((first + b) * TILE, TILE)
        return chol[pl.ds(at, TILE), pl.ds(at, TILE)]

    inverted = [jnp.where(row == col, 1.0 / own_block(b), 0.0) for b in range(share)]
    size = 1
    while size < TILE:
        below = (row // size == col // size + 1) & (row // (2 * size) == col // (2 * size))
        for b in range(share):
            off = jnp.where(below, own_block(b), 0.0)
            if size == 1:
                on_row = jnp.sum(inverted[b], axis=1, keepdims=True)
                on_col = jnp.sum(inverted[b], axis=0, keepdims=True)
                change = on_row * off * on_col
            else:
                change = dot_square(dot_square(inverted[b], off), inverted[b])
            inverted[b] = inverted[b] - change
        size *= 2
    for b in range(share):
        inverse[first + b] = inverted[b]

    shares = inverse.at[pl.ds(first, share)]
    shared = remote(shares, shares, share_sems.at[0], share_sems.at[1], partner)
    shared.start()

    def pass_on(k, h):
        owner = near(k)
        to = left_last if k == half - 1 else left
        hop(k, h, points.at[owner], owner, left).wait_recv()
        hop(k, h, points.at[owner], owner, to).start()

    def pass_on_any(k):
        owner = near(k)
        for h in range(2):
            hop(k, h, points.at[owner], owner, left).wait_recv()

        @pl.when(k < half - 1)
        def _():
            for h in range(2):
                hop(k, h, points.at[owner], owner, left).start()

        @pl.when(k == half - 1)
        def _():
            for h in range(2):
                hop(k, h, points.at[owner], owner, left_last).start()

    own_slot, side_slot, across_slot = 2 * half - 1, 2 * half, 2 * half - 2

    remote(points_ref, points.at[partner], own_sems.at[0], own_sems.at[1], partner).wait_recv()
    side_aug[0:feat, :] = points[partner]
    side_aug[feat:, :] = norm_rows(points[partner], True)
    def total_to(to):
        return remote(ag.at[mine], ag.at[mine], ag_sems.at[0, to], ag_sems.at[1, mine], to)

    @pl.when(adds)
    def _():
        rs_recv[me] = rs_send[mine]
        others(lambda src: remote(
            rs_send.at[0], rs_recv.at[src], rs_sems.at[0, 0], rs_sems.at[1, src], src).wait_recv())
        ag[mine] = jnp.sum(rs_recv[...], axis=0)
        others(lambda to: total_to(to).start())

    def all_square_to(to):
        return remote(square_all, square_all, all_sems.at[0, to], all_sems.at[1, 0], to)

    @pl.when(me == base)
    def _():
        others(lambda src: remote(
            square_buf.at[src], square_buf.at[src], square_sems.at[0], square_sems.at[1 + src], src).wait_recv())
        square_all[...] = jnp.sum(square_buf[...], axis=0)
        others(lambda to: all_square_to(to).start())

    if half > 1:
        pass_on(1, 0)
    if keep:
        make_left(points_ref)
        make_block(own_slot, own_aug)

    other = inverse.at[pl.ds(share - first, share)]
    remote(other, other, share_sems.at[0], share_sems.at[1], partner).wait_recv()
    for b in range(groups):
        upper_block, lower_block = inverse[2 * b], inverse[2 * b + 1]
        at, end = b * GROUP, (b + 1) * GROUP
        off = chol[at + TILE:end, at:at + TILE]
        change = dot_square(dot_square(lower_block, off), upper_block)
        zero = jnp.zeros_like(upper_block)
        whole = jnp.concatenate(
            [jnp.concatenate([upper_block, zero], axis=1), jnp.concatenate([-change, lower_block], axis=1)], axis=0
        )
        store_pair(inverse_parts, (b,), whole)
        if b > 0:
            store_pair(chol_parts, (slice(at, end), slice(0, at)), chol[at:end, :at])

    def make_pair(k, slot):
        make_left(points.at[near(k)])
        make_block(slot, own_aug)
        make_block(slot + 1, side_aug)

    if half > 1:
        pass_on(1, 1)
    if keep:
        make_left(points.at[partner])
        make_block(side_slot, own_aug)
        if half > 1:
            make_pair(1, 0)
    if half > 2:
        pass_on(2, 0)
    each_tile(lambda q: remote(ag.at[q], ag.at[q], ag_sems.at[0, me], ag_sems.at[1, q], base + q).wait_recv())
    for q in range(tiles):
        work[:, q * TILE:(q + 1) * TILE] = ag[q]
    pieces = [work[:, b * GROUP:(b + 1) * GROUP] for b in range(groups)]

    def block_parts(i, j):
        rows, cols = slice(i * GROUP, (i + 1) * GROUP), slice(j * GROUP, (j + 1) * GROUP)
        return [chol_parts[term, rows, cols] for term in range(2)]

    def inverse_of(b):
        return [inverse_parts[term, b] for term in range(2)]

    for b in range(groups):
        pieces[b] = dot_pair(pieces[b], inverse_of(b), dot_nt)
        for i in range(b + 1, groups):
            pieces[i] = pieces[i] - dot_pair(pieces[b], block_parts(i, b), dot_nt)
    halfway = jnp.concatenate(pieces, axis=1)
    if half > 2:
        pass_on(2, 1)
    for b in reversed(range(groups)):
        pieces[b] = dot_pair(pieces[b], inverse_of(b), dot_nn)
        for j in reversed(range(b)):
            pieces[j] = pieces[j] - dot_pair(pieces[b], block_parts(b, j), dot_nn)
    coeffs = jnp.concatenate(pieces, axis=1)

    ridge = ridge_ref[...]
    @pl.when(me != base)
    def _():
        all_square_to(base).wait_recv()

    square = to_column(square_all[...])
    inner = (square - jnp.sum(halfway * halfway, axis=1, keepdims=True)) / ridge
    inner_out[...] = to_row(inner, TILE)[:, :outs]
    residual = residual_ref[...]
    precond = (residual - dot_pair(coeffs, [cross.at[term][...] for term in range(2)], dot_nt)) / ridge
    direction_new = precond + (inner / to_column(rz_ref[...])) * direction_ref[...]
    direction_out[...] = direction_new
    dirs[me] = direction_new.astype(jnp.bfloat16)

    def copy_out(at, src, dst):
        return pltpu.make_async_copy(src, dst, out_sems.at[at])

    direction_copy = copy_out(0, direction_out, direction_hbm)
    inner_copy = copy_out(1, inner_out, inner_hbm)
    image_copy = copy_out(2, image_out, image_hbm)
    alpha_copy = copy_out(3, alpha_out, alpha_hbm)
    direction_copy.start()
    inner_copy.start()

    def dir_to(to):
        return remote(dirs.at[me], dirs.at[to], dir_sems.at[0, to], dir_sems.at[1, me], to)

    def send_dir(to):
        remote(dirs.at[me], dirs.at[me], dir_sems.at[0, to], dir_sems.at[1, me], to).start()

    def wait_dir(src):
        remote(dirs.at[me], dirs.at[src], dir_sems.at[0, src], dir_sems.at[1, src], src).wait_recv()

    send_dir(taker)
    lax.fori_loop(1, half, lambda k, carry: (send_dir(back(half - k)), carry)[1], 0)
    send_dir(partner)
    if keep and half > 3:
        pass_on(3, 0)

    def wait_across():
        for h in range(2):
            hop(0, h, points.at[across], across, left).wait_recv()

    acc[...] = jnp.zeros_like(acc)

    def forward(owner, slot, side):
        acc[1] += dot_nn(dirs[owner], kernel_store[slot])
        if side:
            acc[2] += dot_nn(dirs[owner], kernel_store[slot + 1])

    def image_to(k, owner):
        return remote(img_send.at[k], img_recv.at[k], img_sems.at[0, k], img_sems.at[1, k], owner)

    def backward(k, owner, slot, side):
        total = dot_nt(dirs[me], kernel_store[slot])
        if side:
            total = total + dot_nt(dirs[partner], kernel_store[slot + 1])
        img_send[k] = total
        image_to(k, owner).start()
        return total

    def at_own(slot):
        acc[0] += dot_nn(dirs[me], kernel_store[slot])

    def at_side(slot):
        acc[0] += dot_nn(dirs[partner], kernel_store[slot])

    early = 3

    def terms_behind(total, owner):
        acc[3] += total * dirs[owner].astype(jnp.float32)

    if keep:
        for k in range(2, half):
            if k > 3:
                pass_on(k, 0)
                pass_on(k, 1)
            make_pair(k, 2 * (k - 1))
            if k == 2 and half > 3:
                pass_on(3, 1)
            if k == 2:
                wait_dir(partner)
            if k >= early:
                sent = backward(k - 1, near(k), 2 * (k - 1), True)
                wait_dir(near(k))
                terms_behind(sent, near(k))
        if half < 3:
            wait_dir(partner)
        at_own(own_slot)
        at_side(side_slot)

        def ahead(k, carry):
            wait_dir(near(k))
            forward(near(k), 2 * (k - 1), True)
            return carry

        lax.fori_loop(1, min(half, early), ahead, 0)
        low = dirs[partner].astype(jnp.float32)
        acc[3] += direction_out[...] * acc[1] + low * acc[2]
        wait_across()
        make_left(points.at[across])
        make_block(across_slot, own_aug)
        sent = backward(half - 1, across, across_slot, False)
        wait_dir(across)
        terms_behind(sent, across)
    else:
        make_left(points_ref)
        make_block(0, own_aug)
        at_own(0)
        make_left(points.at[partner])
        make_block(0, own_aug)
        wait_dir(partner)
        at_side(0)

        def both(k, carry):
            @pl.when(k > 2)
            def _():
                pass_on_any(k)

            make_pair(k, 0)
            backward(k - 1, near(k), 0, True)
            wait_dir(near(k))
            forward(near(k), 0, True)
            return carry

        lax.fori_loop(1, half, both, 0)
        wait_across()
        make_left(points.at[across])
        make_block(0, own_aug)
        backward(half - 1, across, 0, False)
        wait_dir(across)
        forward(across, 0, False)
        low = dirs[partner].astype(jnp.float32)
        acc[3] = direction_out[...] * acc[1] + low * acc[2]

    direction_new = direction_out[...]
    own_terms = direction_new * (acc[0] + ridge * direction_new) + 2.0 * acc[3]
    curv_buf[me] = to_row(jnp.sum(own_terms, axis=1, keepdims=True), TILE)
    send_all(lambda to: curv_buf.at[me], curv_buf, curv_sems)

    if keep:
        last = min(half, early)

        def behind(i, carry):
            k = last - i
            backward(k - 1, near(k), 2 * (k - 1), True)
            return carry

        lax.fori_loop(1, last, behind, 0)
        for k in range(early, half):
            forward(near(k), 2 * (k - 1), True)

    side_send = remote(acc.at[2], side_recv, side_sems.at[0], side_sems.at[1], partner)
    side_send.start()

    if keep:
        forward(across, across_slot, False)

    each_tile(lambda q: tile_to(q).wait_send())

    @pl.when(me != base)
    def _():
        square_to(base).wait_send()

    @pl.when(me == base)
    def _():
        others(lambda to: all_square_to(to).wait_send())

    @pl.when(adds)
    def _():
        others(lambda to: total_to(to).wait_send())

    shared.wait_send()
    for copy in own_left:
        copy.wait_send()
    own_side.wait_send()

    def relay_drain(k, carry):
        for h in range(2):
            hop(k, h, points.at[near(k)], near(k), left).wait_send()
        return carry

    lax.fori_loop(1, half, relay_drain, 0)

    def dir_drain(k, carry):
        dir_to(back(k)).wait_send()
        return carry

    lax.fori_loop(1, half, dir_drain, 0)
    dir_to(taker).wait_send()
    dir_to(partner).wait_send()

    side_send.wait_recv()
    image = acc[0] + acc[1] + ridge * direction_new + side_recv[...]
    for k in range(half):
        image_to(k, across).wait_recv()
        image = image + img_recv[k]
    image_out[...] = image
    image_copy.start()

    wait_all(lambda to: curv_buf.at[me], curv_buf, curv_sems)
    alpha_out[...] = inner_out[...] / jnp.sum(curv_buf[...], axis=0)[:, :outs]
    alpha_copy.start()
    drain(lambda to: curv_buf.at[me], curv_buf, curv_sems)
    side_send.wait_send()
    for k in range(half):
        image_to(k, across).wait_send()
    direction_copy.wait()
    inner_copy.wait()
    image_copy.wait()
    alpha_copy.wait()


def finish(
    image_ref,
    direction_ref,
    inner_ref,
    alpha_ref,
    solution_ref,
    residual_ref,
    solution_out,
    residual_out,
    direction_out,
    inner_out,
):
    alpha = to_column(alpha_ref[...])
    direction = direction_ref[...]
    solution_out[...] = solution_ref[...] + alpha * direction
    residual_out[...] = residual_ref[...] - alpha * image_ref[...]
    direction_out[...] = direction
    inner_out[...] = inner_ref[...]


def solution(mesh):
    n = mesh.shape["rows"]

    def local(points, landmarks, chol, ridge, solution, residual, direction, rz_prev):
        feat, own = points.shape
        land = landmarks.shape[1]
        outs = residual.shape[0]
        keep = n <= STORED_BLOCKS
        half = n // 4
        tiles = land // TILE
        f32, bf16 = jnp.float32, jnp.bfloat16
        vmem = pl.BlockSpec(memory_space=pltpu.VMEM)
        wide = jax.ShapeDtypeStruct((outs, own), f32)
        thin = jax.ShapeDtypeStruct((1, outs), f32)
        dma = pltpu.SemaphoreType.DMA
        anywhere = pl.BlockSpec(memory_space=pl.ANY)
        results = pl.pallas_call(
            functools.partial(kernel, n, keep),
            out_shape=(wide, wide, thin, thin),
            in_specs=[
                vmem,
                vmem,
                pl.BlockSpec(memory_space=pl.ANY),
                vmem,
                vmem,
                vmem,
                vmem,
            ],
            out_specs=(anywhere,) * 4,
            scratch_shapes=[
                pltpu.VMEM((land, land), f32),
                pltpu.VMEM((2, land, land), bf16),
                pltpu.VMEM((2, land // GROUP, GROUP, GROUP), bf16),
                pltpu.VMEM((tiles, TILE, TILE), f32),
                pltpu.VMEM((n, feat, own), bf16),
                pltpu.VMEM((feat + 16, own), bf16),
                pltpu.VMEM((feat + 16, own), bf16),
                pltpu.VMEM((feat + 16, own), bf16),
                pltpu.VMEM((2, own, land), bf16),
                pltpu.VMEM((2 * half + 1 if keep else 2, own, own), bf16),
                pltpu.VMEM((tiles, outs, TILE), f32),
                pltpu.VMEM((n, outs, TILE), f32),
                pltpu.VMEM((tiles, outs, TILE), f32),
                pltpu.VMEM((outs, land), f32),
                pltpu.VMEM((outs, land), f32),
                pltpu.VMEM((n, outs, own), bf16),
                pltpu.VMEM((4, outs, own), f32),
                pltpu.VMEM((outs, own), f32),
                pltpu.VMEM((half, outs, own), f32),
                pltpu.VMEM((half, outs, own), f32),
                pltpu.VMEM((n, 1, TILE), f32),
                dma,
                dma((2, n)),
                dma((2, n)),
                dma((2, n)),
                dma((2, n)),
                dma((2, half)),
                dma((2,)),
                dma((n, 2)),
                dma((half, 2)),
                dma((2,)),
                dma((2,)),
                pltpu.VMEM((outs, own), f32),
                pltpu.VMEM((outs, own), f32),
                pltpu.VMEM((1, outs), f32),
                pltpu.VMEM((1, outs), f32),
                dma((4,)),
                pltpu.VMEM((n, 1, TILE), f32),
                pltpu.VMEM((1, TILE), f32),
                dma((1 + n,)),
                dma((2, n)),
            ],
            compiler_params=pltpu.CompilerParams(
                collective_id=0, has_side_effects=True, vmem_limit_bytes=LIMIT * 1024 * 1024
            ),
            name="cg_step",
        )(points, landmarks, chol, ridge.reshape(1, 1), residual, direction, rz_prev.reshape(1, outs))
        results = pl.pallas_call(
            finish,
            out_shape=(wide, wide, wide, thin),
            in_specs=[vmem] * 6,
            out_specs=(vmem,) * 4,
            name="finish",
        )(*results, solution, residual)
        return (results[0], results[1], results[2], results[3].reshape(outs))

    wide_spec = P(None, ("groups", "rows"))
    in_specs = (
        wide_spec,
        P(None, "groups"),
        P("groups", None),
        P("groups"),
        wide_spec,
        wide_spec,
        wide_spec,
        P("groups"),
    )
    out_specs = (wide_spec, wide_spec, wide_spec, P("groups"))
    return jax.shard_map(local, mesh=mesh, in_specs=in_specs, out_specs=out_specs, check_vma=False)
```
